32 devices in a mesh: seq: 16 (over z, x, core), head: 2 (over y).
Axes of the slice: x: 2, y: 2, z: 4, core: 2. Of those that a mesh axis runs over, the one named last changes fastest.
Arguments:
- queries: bfloat16 [16384, 4096], P('seq', 'head'), may hold values from -90 to 90
- keys: bfloat16 [16384, 4096], P('seq', 'head'), may hold values from -50 to 50
- values: bfloat16 [16384, 4096], P('seq', 'head'), may hold values from -6 to 6
- cluster_ids: int32 [16384, 32], P('seq', 'head'), may hold values from 0 to 255, as said below
- out_weight: bfloat16 [4096, 4096], P('head', 'seq'), may hold values from -2.390625 to 2.390625
Outputs:
- mixed: bfloat16 [16384, 4096], P('seq', 'head')
The draws below stay inside these ranges and needn't reach their ends.
Inputs may be any that keep to these rules, and one draw needn't show every extreme that they name: `cluster_ids`: in every head each of the 256 clusters holds at least one token.
All inputs are finite; a program needn't handle non-finite values.
Results may differ from the reference program's by a relative error of at most 0.01.
Values may be sent and summed in bfloat16 or wider, within the bound.
A program may use at most 128 MiB of HBM per device.

```python
import jax
import jax.numpy as jnp
from jax import lax

D = 4096
HEADS = 32
HDIM = 128
CLUSTERS = 256
TOK_DEV = 1024
TOKENS = 16384
HD = 4096
N_SEQ = 16
N_HEAD = 2


def label_table(key):
    base_key = jax.random.fold_in(key, 11)
    first_key, second_key = jax.random.split(base_key)
    labels = jax.random.randint(first_key, (TOKENS, HEADS), 0, CLUSTERS, dtype=jnp.int32)
    head_keys = jax.random.split(second_key, HEADS)

    def place(head_key, column):
        chosen_rows = jax.random.permutation(head_key, TOKENS)[:CLUSTERS]
        return column.at[chosen_rows].set(jnp.arange(CLUSTERS, dtype=jnp.int32))
    return jax.vmap(place, in_axes=(0, 1), out_axes=1)(head_keys, labels)


def draw_cluster_ids(key, part):
    return label_table(key)


def draw_queries(key, part):
    labels = label_table(key)
    centre_key, jitter_key = jax.random.split(jax.random.fold_in(key, 12))
    centre = 2.0 * jnp.clip(jax.random.normal(centre_key, (HEADS, CLUSTERS, HDIM), jnp.float32), -4.0, 4.0)
    member_centre = jax.vmap(lambda table, column: table[column], in_axes=(0, 1), out_axes=1)(centre, labels)
    jitter = jnp.clip(jax.random.normal(jitter_key, (TOKENS, HEADS, HDIM), jnp.float32), -4.0, 4.0)
    query_rows = member_centre + jitter
    return query_rows.reshape(TOKENS, HEADS * HDIM).astype(jnp.bfloat16)


def draw_keys(key, part):
    row_key = jax.random.fold_in(key, 21)
    key_rows = jnp.clip(jax.random.normal(row_key, (TOKENS, HEADS, HDIM), jnp.float32), -5.0, 5.0)
    return key_rows.reshape(TOKENS, HEADS * HDIM).astype(jnp.bfloat16)


def levels(rng, dims, cuts, smallest, high):
    def one(dim, blocks):
        steps = jax.random.uniform(jax.random.fold_in(jax.random.fold_in(rng, 6), dim), (blocks,), jnp.float32, smallest / len(cuts), high / len(cuts))
        return jnp.repeat(jnp.exp(steps), dims[dim] // blocks).reshape((-1,) + (1,) * (len(dims) - dim - 1))

    loudness = one(*cuts[0])
    for cut in cuts[1:]:
        loudness = loudness * one(*cut)
    return loudness


def centred(rng, extent, scale, limit, pieces=(), held_as=jnp.bfloat16):
    entries = jax.random.normal(rng, extent, jnp.float32) * scale
    if len(pieces) > 0:
        entries = levels(rng, extent, pieces, -0.22, 0.18) * entries
    return jnp.clip(entries, min=-limit, max=limit).astype(held_as)


def setup_inputs(seed: int = 0) -> dict:
    streams_of = jax.random.split(jax.random.key(seed), 6)
    queries = draw_queries(jax.random.fold_in(streams_of[5], 71), 0)
    keys = draw_keys(jax.random.fold_in(streams_of[5], 71), 0)
    values = centred(streams_of[2], (TOKENS, HD), 1.0, 6.0, ((0, 16), (1, 2)))
    cluster_ids = draw_cluster_ids(jax.random.fold_in(streams_of[5], 71), 0)
    out_weight = centred(streams_of[4], (HD, D), 0.4, 2.390625, ((0, 2), (1, 16)))
    return dict(queries=queries, keys=keys, values=values, cluster_ids=cluster_ids, out_weight=out_weight)


def per_head(head, queries, keys, values, cluster_ids):
    first_col = (head * HDIM).astype(jnp.int32)
    labels = lax.dynamic_slice_in_dim(cluster_ids, head.astype(jnp.int32), 1, 1)[:, 0]
    query_rows = lax.dynamic_slice_in_dim(queries, first_col, HDIM, 1).astype(jnp.float32)
    key_rows = lax.dynamic_slice_in_dim(keys, first_col, HDIM, 1).astype(jnp.float32)
    value_rows = lax.dynamic_slice_in_dim(values, first_col, HDIM, 1).astype(jnp.float32)
    member = (labels[:, None] == jnp.arange(CLUSTERS, dtype=jnp.int32)[None, :]).astype(jnp.float32)
    totals = jnp.dot(member.T, query_rows, precision=lax.Precision.HIGHEST)
    counts = jnp.sum(member, axis=0)
    centre = (totals / counts[:, None]).astype(jnp.bfloat16)
    centre = lax.optimization_barrier(centre).astype(jnp.float32)
    key_blocks = key_rows.reshape(N_SEQ, TOK_DEV, HDIM)
    value_blocks = value_rows.reshape(N_SEQ, TOK_DEV, HDIM)
    scores = jnp.einsum("cd,btd->cbt", centre, key_blocks, precision=lax.Precision.HIGHEST) * (1.0 / (HDIM ** 0.5))
    block_peak = jnp.max(scores, axis=2)
    weights = jnp.exp(scores - block_peak[:, :, None]).astype(jnp.bfloat16)
    weights = lax.optimization_barrier(weights).astype(jnp.float32)
    block_mass = jnp.sum(weights, axis=2)
    block_output = jnp.einsum("cbt,btd->cbd", weights, value_blocks, precision=lax.Precision.HIGHEST)
    global_peak = jnp.max(block_peak, axis=1)
    factor = jnp.exp(block_peak - global_peak[:, None])
    output_sum = jnp.sum(factor[:, :, None] * block_output, axis=1)
    mass_sum = jnp.sum(factor * block_mass, axis=1)
    centroid_out = (output_sum / mass_sum[:, None]).astype(jnp.bfloat16)
    return jnp.take(centroid_out, labels, axis=0)


def reference(queries, keys, values, cluster_ids, out_weight):
    def one_head(head):
        return per_head(head, queries, keys, values, cluster_ids)

    attended = lax.map(one_head, jnp.arange(HEADS, dtype=jnp.int32))
    attended = jnp.transpose(attended, (1, 0, 2)).reshape(TOKENS, HEADS * HDIM)
    group_rows = (HEADS * HDIM) // N_HEAD
    summed = jnp.zeros((TOKENS, D), jnp.float32)
    for group in range(N_HEAD):
        term = jnp.dot(attended[:, group * group_rows:(group + 1) * group_rows].astype(jnp.float32),
                       out_weight[group * group_rows:(group + 1) * group_rows, :].astype(jnp.float32),
                       precision=lax.Precision.HIGHEST)
        term = lax.optimization_barrier(term.astype(jnp.bfloat16))
        summed = summed + term.astype(jnp.float32)
    return summed.astype(jnp.bfloat16)
```

```python
import functools
import math

import jax
import jax.numpy as jnp
from jax import lax
from jax.experimental import pallas as pl
from jax.experimental.pallas import tpu as pltpu
from jax.sharding import PartitionSpec as P

HDIM = 128
CLUSTERS = 256
LANES = 128
STAT = 8
MASS = 4
CORES = 2
PIECES = 16
MESH = pl.DeviceIdType.MESH
F32 = jnp.float32
BF16 = jnp.bfloat16
SCALE = math.log2(math.e) / math.sqrt(HDIM)


def grid_of(n):
    chips = n // CORES
    bits = chips.bit_length() - 1
    a = 1 << ((bits + 1) // 2)
    return chips, a, chips // a


def columns_of(row, block):
    return jnp.broadcast_to(row, (LANES, LANES)).T[:block]


def row_of(column):
    block = column.shape[0]
    return jnp.concatenate([column] * (LANES // block), axis=0).T[:1]


def one_hot(ids_row):
    labels = lax.broadcasted_iota(jnp.int32, (CLUSTERS, ids_row.shape[1]), 0).astype(BF16)
    return jnp.where(labels == ids_row.astype(BF16), jnp.ones((), BF16), jnp.zeros((), BF16))


def fused_kernel(
    n, heads_n, ids_ref, q_ref, k_ref, v_ref, w_ref, cev, wall, ids_out,
    qv, kv, vv, line, accf, stat, outb, recvb, statr, mb, mc, rx, rxc, full,
    load_sem, own_sem, id_send, id_recv, ex_send, ex_recv, rs_send, rs_recv, ag_send, ag_recv,
    sib_send, sib_recv, a2_send, a2_recv, y2_send, y2_recv, s2_send, s2_recv,
    wz_send, wz_recv, wy_send, wy_recv, wx_send, wx_recv, wc_send, wc_recv,
):
    chips, na, nb = grid_of(n)
    heads, tokens = ids_ref.shape
    per = heads // na
    rows = mb.shape[-2]
    slices = CLUSTERS // rows
    block = min(rows, LANES)
    blocks = rows // block
    width = per * HDIM
    height = w_ref.shape[0] // PIECES
    seq = lax.axis_index("seq")
    head = lax.axis_index("head")
    core = lax.rem(seq, CORES)
    chip = seq // CORES
    za = chip // nb
    xb = lax.rem(chip, nb)
    wide = na // heads_n
    half = za // wide
    spot = lax.rem(za, wide)
    sibling = {"seq": chip * CORES + 1 - core}

    def at_chip(target):
        return {"seq": target * CORES + core}

    def at_head(step):
        return {"head": lax.rem(head + step, heads_n)}

    def remote(src, dst, send, recv, where):
        return pltpu.make_async_remote_copy(
            src_ref=src, dst_ref=dst, send_sem=send, recv_sem=recv, device_id=where, device_id_type=MESH
        )

    def chip_to(j):
        return lax.rem(chip + j, chips)

    def chip_from(j):
        return lax.rem(chip - j + chips, chips)

    def loads(g, number):
        src, dst = ((q_ref, qv), (k_ref, kv), (v_ref, vv))[number]
        return pltpu.make_async_copy(
            src.at[:, pl.ds(pl.multiple_of(g * width, width), width)], dst.at[g], load_sem.at[number, g]
        )

    for step in range(1, na + 1):
        loads(lax.rem(za + step, na), 0).start()

    barrier = pltpu.get_barrier_semaphore()
    targets = [sibling] + [at_chip(chip_to(j)) for j in range(1, chips)]
    targets += [at_head(step) for step in range(1, heads_n)]
    for target in targets:
        pl.semaphore_signal(barrier, inc=1, device_id=target, device_id_type=MESH)

    own_ids = pltpu.make_async_copy(ids_ref, ids_out.at[head], own_sem.at[1])
    own_ids.start()
    mine = half == head

    @pl.when(mine)
    def _():
        pltpu.make_async_copy(w_ref, wall.at[core, xb, spot, head], own_sem.at[0]).start()

    @pl.when(jnp.logical_not(mine))
    def _():
        pltpu.make_async_copy(w_ref, line.at[half, spot], own_sem.at[0]).start()

    for step in range(na):
        for number in (1, 2):
            loads(lax.rem(za + step, na), number).start()
    pl.semaphore_wait(barrier, len(targets))

    def span(p):
        return pl.ds(p * height, height)

    def along(step, p, kept):
        there = lax.rem(za + step, na) * nb + xb
        dst = wall.at[core, xb, spot, head, span(p)] if kept else line.at[half, spot, span(p)]
        return remote(
            w_ref.at[span(p)], dst, wz_send.at[step - 1, p], wz_recv.at[step - 1, p], at_chip(there)
        )

    def to_group(step, p):
        return remote(
            line.at[lax.rem(head + step, heads_n), :, span(p)],
            wall.at[core, xb, :, head, span(p)],
            wy_send.at[step - 1, p], wy_recv.at[step - 1, p], at_head(step),
        )

    def across(step, p):
        part = wall.at[core, xb, :, :, span(p)]
        there = za * nb + lax.rem(xb + step, nb)
        return remote(part, part, wx_send.at[step - 1, p], wx_recv.at[step - 1, p], at_chip(there))

    def over(p):
        part = wall.at[core, :, :, :, span(p)]
        return remote(part, part, wc_send.at[p], wc_recv.at[p], sibling)

    def stage_one(p):
        @pl.when(mine)
        def _():
            for step in range(1, na):
                along(step, p, True).start()

        @pl.when(jnp.logical_not(mine))
        def _():
            for step in range(1, na):
                along(step, p, False).start()

    def stage_two(p):
        for step in range(1, na):
            along(step, p, True).wait_recv()
        for step in range(1, heads_n):
            to_group(step, p).start()

    def stage_three(p):
        for step in range(1, heads_n):
            to_group(step, p).wait_recv()
        for step in range(1, nb):
            across(step, p).start()

    def stage_four(p):
        for step in range(1, nb):
            across(step, p).wait_recv()
        over(p).start()

    stages = (stage_one, stage_two, stage_three, stage_four)

    def tick(t):
        for number, stage in enumerate(stages):
            p = t - number
            if isinstance(p, int):
                if 0 <= p < PIECES:
                    stage(p)
            else:
                pl.when((p >= 0) & (p < PIECES))(functools.partial(stage, p))

    tick(0)
    id_copies = [
        remote(ids_ref, ids_out.at[head], id_send.at[step - 1], id_recv.at[step - 1], at_head(step))
        for step in range(1, heads_n)
    ]
    for copy in id_copies:
        copy.start()

    def exchange(phase, g):
        return [
            remote(
                outb.at[phase, g], recvb.at[phase, g],
                ex_send.at[phase, g, 0], ex_recv.at[phase, g, 0], sibling,
            ),
            remote(
                stat.at[phase, 1 - core, g], statr.at[phase, g],
                ex_send.at[phase, g, 1], ex_recv.at[phase, g, 1], sibling,
            ),
        ]

    def deliver(phase, j, number):
        target = chip_to(j)
        g, b = target // nb, lax.rem(target, nb)
        src, dst = ((mb, rx), (mc, rxc))[number]
        return remote(
            src.at[phase, g, b], dst.at[phase, j],
            rs_send.at[phase, j, number], rs_recv.at[phase, j, number], at_chip(target),
        )

    def hand_over(phase, g):
        for b in range(nb):
            outb[phase, g, b] = accf[1 - core, g, b].astype(BF16)
        for copy in exchange(phase, g):
            copy.start()

    def send_on(phase, g):
        for b in range(nb):
            j = lax.rem(g * nb + b - chip + chips, chips)

            @pl.when(j != 0)
            def _(j=j):
                for number in range(2):
                    deliver(phase, j, number).start()

    def places(i):
        for s in range(slices):
            number = i * slices + s
            yield slice(s * rows, (s + 1) * rows), number // CORES, number % CORES

    def tile_of(pieces):
        filled = [None] * STAT
        for at, column in pieces:
            for b in range(blocks):
                filled[at + b] = row_of(column[b * block : (b + 1) * block])
        blank = jnp.zeros((1, LANES), F32)
        return jnp.concatenate([blank if row is None else row for row in filled], axis=0)

    ones = jnp.ones((tokens, LANES), BF16)

    def merge_sums(g):
        for copy in exchange(0, g):
            copy.wait()
        for b in range(nb):
            total = accf[core, g, b] + recvb[0, g, b].astype(F32)
            accf[core, g, b] = total
            mb[0, g, b] = total.astype(BF16)
            mc[0, g, b] = stat[0, core, g, b] + statr[0, g, b]
        send_on(0, g)

    def sum_group(k, carry):
        g = lax.rem(za + 1 + k, na)
        loads(g, 0).wait()
        for i in range(per):
            member = one_hot(ids_ref[pl.ds(g * per + i, 1), :])
            both = jnp.concatenate([qv[g, :, i * HDIM : (i + 1) * HDIM], ones], axis=1)
            result = jnp.dot(member, both, preferred_element_type=F32)
            for where, b, c in places(i):
                accf[c, g, b] = result[where, :HDIM]
                stat[0, c, g, b] = tile_of([(0, result[where, HDIM:])])
        hand_over(0, g)

        @pl.when(k > 0)
        def _():
            merge_sums(lax.rem(za + k, na))

        return carry

    lax.fori_loop(0, na, sum_group, 0)
    pltpu.make_async_copy(w_ref, line.at[half, spot], own_sem.at[0]).wait()
    tick(1)
    merge_sums(za)
    tick(2)

    for j in range(1, chips):
        for number in range(2):
            deliver(0, j, number).wait()
        accf[core, za, xb] = accf[core, za, xb] + rx[0, j].astype(F32)
        mc[0, za, xb] = mc[0, za, xb] + rxc[0, j]
        if j == chips // 2:
            tick(3)
    for b in range(blocks):
        where = slice(b * block, (b + 1) * block)
        count = columns_of(mc[0, za, xb, b : b + 1, :], block)
        full[chip, core, where, :] = (accf[core, za, xb, where, :] / count).astype(BF16)

    def spread(j):
        part = full.at[chip, core]
        return remote(part, part, ag_send.at[j], ag_recv.at[j], at_chip(chip_to(j)))

    def share(g):
        part = full.at[pl.ds(g * nb, nb), core]
        return remote(part, part, sib_send.at[g], sib_recv.at[g], sibling)

    def pass_group(g):
        for b in range(nb):
            j = lax.rem(chip - g * nb - b + chips, chips)

            @pl.when(j != 0)
            def _(j=j):
                spread(j).wait_recv()

        share(g).start()

    for j in range(1, chips):
        spread(j).start()
    tick(4)
    pass_group(za)

    def merge_parts(g):
        for copy in exchange(1, g):
            copy.wait()
        for b in range(nb):
            left, right = stat[1, core, g, b], statr[1, g, b]
            peak = jnp.maximum(left[:MASS], right[:MASS])
            scale_l = jnp.exp2((left[:MASS] - peak) * SCALE)
            scale_r = jnp.exp2((right[:MASS] - peak) * SCALE)
            mass = left[MASS:] * scale_l + right[MASS:] * scale_r
            mc[1, g, b] = jnp.concatenate([peak, mass], axis=0)
            for x in range(blocks):
                where = slice(x * block, (x + 1) * block)
                total = accf[core, g, b, where, :] * columns_of(scale_l[x : x + 1], block)
                total += recvb[1, g, b, where, :].astype(F32) * columns_of(scale_r[x : x + 1], block)
                accf[core, g, b, where, :] = total
                mb[1, g, b, where, :] = total.astype(BF16)
        send_on(1, g)

    def attend_group(k, carry):
        g = lax.rem(za + k, na)
        following = lax.rem(g + 1, na)

        @pl.when((k >= 1) & (k + 1 < na))
        def _():
            pass_group(following)

        share(g).wait()
        loads(g, 1).wait()
        loads(g, 2).wait()
        for i in range(per):
            cols = slice(i * HDIM, (i + 1) * HDIM)
            centre = jnp.concatenate([full[g * nb + b, c] for _, b, c in places(i)], axis=0)
            scores = lax.dot_general(
                centre, kv[g, :, cols], (((1,), (1,)), ((), ())), preferred_element_type=F32
            )
            peak = jnp.max(scores, axis=1, keepdims=True)
            weights = jnp.exp2((scores - peak) * SCALE).astype(BF16)
            both = jnp.concatenate([vv[g, :, cols], ones], axis=1)
            result = jnp.dot(weights, both, preferred_element_type=F32)
            peak = jnp.broadcast_to(peak, (CLUSTERS, LANES))
            for where, b, c in places(i):
                accf[c, g, b] = result[where, :HDIM]
                stat[1, c, g, b] = tile_of([(0, peak[where]), (MASS, result[where, HDIM:])])
        hand_over(1, g)
        tick(5 + k)

        @pl.when(k == 0)
        def _():
            pass_group(following)

        @pl.when(k > 0)
        def _():
            merge_parts(lax.rem(g - 1 + na, na))

        return carry

    lax.fori_loop(0, na, attend_group, 0)
    t = 5 + na
    tick(t)
    merge_parts(lax.rem(za + na - 1, na))

    for j in range(1, chips):
        deliver(1, j, 1).wait()
    stats = [mc[1, za, xb]] + [rxc[1, j] for j in range(1, chips)]
    top = functools.reduce(jnp.maximum, [s[:MASS] for s in stats])
    scales = [jnp.exp2((s[:MASS] - top) * SCALE) for s in stats]
    mass = sum(s[MASS:] * scale for s, scale in zip(stats, scales))
    tick(t + 1)
    for j in range(chips):
        if j > 0:
            deliver(1, j, 0).wait()
        for x in range(blocks):
            where = slice(x * block, (x + 1) * block)
            column = columns_of(scales[j][x : x + 1], block)
            if j == 0:
                accf[core, za, xb, where, :] = accf[core, za, xb, where, :] * column
            else:
                accf[core, za, xb, where, :] += rx[1, j, where, :].astype(F32) * column
    for x in range(blocks):
        where = slice(x * block, (x + 1) * block)
        total = columns_of(mass[x : x + 1], block)
        cev[head, chip, core, where, :] = (accf[core, za, xb, where, :] / total).astype(BF16)

    def spread_out(j):
        part = cev.at[head, chip, core]
        return remote(part, part, a2_send.at[j], a2_recv.at[j], at_chip(chip_to(j)))

    def cross(step, s):
        part = cev.at[head, s, core]
        return remote(part, part, y2_send.at[step - 1, s], y2_recv.at[step - 1, s], at_head(step))

    def share_out(h, s):
        part = cev.at[h, s, core]
        return remote(part, part, s2_send.at[h, s], s2_recv.at[h, s], sibling)

    for j in range(1, chips):
        spread_out(j).start()
    for step in range(1, heads_n):
        cross(step, chip).start()
    share_out(head, chip).start()
    tick(t + 2)
    for j in range(1, chips):
        s = chip_from(j)
        spread_out(j).wait_recv()
        for step in range(1, heads_n):
            cross(step, s).start()
        share_out(head, s).start()
    for j in range(chips):
        s = chip_from(j)
        for step in range(1, heads_n):
            cross(step, s).wait_recv()
            share_out(lax.rem(head - step + heads_n, heads_n), s).start()
    for late in range(t + 3, PIECES + len(stages) - 1):
        tick(late)

    for copy in id_copies:
        copy.wait()
    own_ids.wait()
    for j in range(1, chips):
        spread(j).wait_send()
        spread_out(j).wait_send()

    def settle(s, carry):
        for h in range(heads_n):
            share_out(h, s).wait()
        for step in range(1, heads_n):
            cross(step, s).wait_send()
        return carry

    lax.fori_loop(0, chips, settle, 0)

    def finish(p, carry):
        for step in range(1, na):
            along(step, p, True).wait_send()
        for step in range(1, heads_n):
            to_group(step, p).wait_send()
        for step in range(1, nb):
            across(step, p).wait_send()
        over(p).wait()
        return carry

    lax.fori_loop(0, PIECES, finish, 0)


def project_kernel(steps, heads_n, ids_ref, centre_ref, w_ref, out_ref, attended):
    step = pl.program_id(0)
    per = centre_ref.shape[0]
    groups = attended.shape[0]

    @pl.when(step < steps)
    def _():
        for i in range(per):
            member = one_hot(ids_ref[pl.ds(step * per + i, 1), :])
            rows = lax.dot_general(
                member, centre_ref[i], (((0,), (0,)), ((), ())), preferred_element_type=F32
            )
            attended[step, :, i * HDIM : (i + 1) * HDIM] = rows.astype(BF16)

    @pl.when(step >= steps)
    def _():
        depth = attended.shape[2]
        each = groups // heads_n
        total = None
        for h in range(heads_n):
            term = None
            for g in range(each):
                part = jnp.dot(
                    attended[h * each + g], w_ref[0, 0, 0, h, g * depth : (g + 1) * depth, :],
                    preferred_element_type=F32,
                )
                term = part if term is None else term + part
            term = term.astype(BF16).astype(F32)
            total = term if total is None else total + term
        out_ref[...] = total.astype(BF16)


def local(queries, keys, values, cluster_ids, out_weight):
    n = lax.axis_size("seq")
    heads_n = lax.axis_size("head")
    chips, na, nb = grid_of(n)
    tokens = queries.shape[0]
    heads = queries.shape[1] // HDIM
    rows = heads * CLUSTERS // n
    width = heads // na * HDIM
    depth, cols = out_weight.shape
    wide = na // heads_n
    ids_t = cluster_ids.T

    vmem = pl.BlockSpec(memory_space=pltpu.VMEM)
    anywhere = pl.BlockSpec(memory_space=pl.ANY)
    dma = pltpu.SemaphoreType.DMA

    def pair(*shape):
        shape = tuple(max(size, 1) for size in shape)
        return [dma(shape), dma(shape)]

    cev, wall, ids_every = pl.pallas_call(
        functools.partial(fused_kernel, n, heads_n),
        out_shape=(
            jax.ShapeDtypeStruct((heads_n, chips, CORES, rows, HDIM), BF16),
            jax.ShapeDtypeStruct((CORES, nb, wide, heads_n, depth, cols), BF16),
            jax.ShapeDtypeStruct((heads_n, heads, tokens), jnp.int32),
        ),
        in_specs=[vmem, anywhere, anywhere, anywhere, anywhere],
        out_specs=(vmem, anywhere, anywhere),
        scratch_shapes=[
            *[pltpu.VMEM((na, tokens, width), BF16) for _ in range(3)],
            pltpu.VMEM((heads_n, wide, depth, cols), BF16),
            pltpu.VMEM((CORES, na, nb, rows, HDIM), F32),
            pltpu.VMEM((2, CORES, na, nb, STAT, LANES), F32),
            pltpu.VMEM((2, na, nb, rows, HDIM), BF16),
            pltpu.VMEM((2, na, nb, rows, HDIM), BF16),
            pltpu.VMEM((2, na, nb, STAT, LANES), F32),
            pltpu.VMEM((2, na, nb, rows, HDIM), BF16),
            pltpu.VMEM((2, na, nb, STAT, LANES), F32),
            pltpu.VMEM((2, chips, rows, HDIM), BF16),
            pltpu.VMEM((2, chips, STAT, LANES), F32),
            pltpu.VMEM((chips, CORES, rows, HDIM), BF16),
            dma((3, na)), dma((2,)),
            *pair(heads_n - 1),
            *pair(2, na, 2), *pair(2, chips, 2), *pair(chips), *pair(na),
            *pair(chips), *pair(heads_n - 1, chips), *pair(heads_n, chips),
            *pair(na - 1, PIECES), *pair(heads_n - 1, PIECES), *pair(nb - 1, PIECES), *pair(PIECES),
        ],
        compiler_params=pltpu.CompilerParams(
            collective_id=0, has_side_effects=True, vmem_limit_bytes=56 << 20
        ),
    )(ids_t, queries, keys, values, out_weight)

    every = heads_n * heads
    per = heads // na
    steps = every // per
    columns = CORES * nb * wide

    def weight_block(i):
        j = jnp.maximum(i - steps, 0)
        return lax.rem(j, CORES), lax.rem(j // CORES, nb), j // (CORES * nb), 0, 0, 0

    return pl.pallas_call(
        functools.partial(project_kernel, steps, heads_n),
        out_shape=jax.ShapeDtypeStruct((tokens, columns * cols), BF16),
        grid=(steps + columns,),
        in_specs=[
            vmem,
            pl.BlockSpec((per, CLUSTERS, HDIM), lambda i: (jnp.minimum(i, steps - 1), 0, 0)),
            pl.BlockSpec((1, 1, 1, heads_n, depth, cols), weight_block),
        ],
        out_specs=pl.BlockSpec((tokens, cols), lambda i: (0, jnp.maximum(i - steps, 0))),
        scratch_shapes=[pltpu.VMEM((steps, tokens, per * HDIM), BF16)],
        compiler_params=pltpu.CompilerParams(vmem_limit_bytes=48 << 20),
    )(ids_every.reshape(every, tokens), cev.reshape(every, CLUSTERS, HDIM), wall)


def solution(mesh):
    return jax.shard_map(
        local,
        mesh=mesh,
        in_specs=(
            P("seq", "head"),
            P("seq", "head"),
            P("seq", "head"),
            P("seq", "head"),
            P("head", "seq"),
        ),
        out_specs=P("seq", "head"),
        check_vma=False,
    )
```

```python
import functools
import math

import jax
import jax.numpy as jnp
from jax import lax
from jax.experimental import pallas as pl
from jax.experimental.pallas import tpu as pltpu
from jax.sharding import PartitionSpec as P

HDIM = 128
CLUSTERS = 256
LANES = 128
STAT = 8
MASS = 4
CORES = 2
PIECES = 16
LAG = 2
BEATS = {'start': (), 'sums': (0, 1, 0, 1), 'owned': (1,), 'centre': (), 'spread': (1,), 'attend': (1, 1, 1, 1), 'parts': (1,), 'stats': (1,), 'merge': (), 'out': (1,), 'near': (), 'far': (), 'gather': (1, 1, 1, 1, 1, 1, 1, 1)}
MESH = pl.DeviceIdType.MESH
F32 = jnp.float32
BF16 = jnp.bfloat16
SCALE = math.log2(math.e) / math.sqrt(HDIM)


def grid_of(n):
    chips = n // CORES
    bits = chips.bit_length() - 1
    a = 1 << ((bits + 1) // 2)
    return chips, a, chips // a


def columns_of(row, block):
    return jnp.broadcast_to(row, (LANES, LANES)).T[:block]


def row_of(column):
    block = column.shape[0]
    return jnp.concatenate([column] * (LANES // block), axis=0).T[:1]


def one_hot(ids_row):
    labels = lax.broadcasted_iota(jnp.int32, (CLUSTERS, ids_row.shape[1]), 0).astype(BF16)
    return jnp.where(labels == ids_row.astype(BF16), jnp.ones((), BF16), jnp.zeros((), BF16))


def fused_kernel(
    n, heads_n, ids_ref, q_ref, k_ref, v_ref, w_ref, out_ref,
    cev, wall, ids_all, outbox, qkv, line, accf, stat, outb, recvb, statr, mb, mc, rx, rxc, full,
    load_sem, own_sem, id_send, id_recv, ex_send, ex_recv, rs_send, rs_recv, ag_send, ag_recv,
    sib_send, sib_recv, a2_send, a2_recv, y2_send, y2_recv, s2_send, s2_recv,
    wz_send, wz_recv, wx_send, wx_recv, wc_send, wc_recv, out_send, out_recv,
):
    chips, na, nb = grid_of(n)
    heads, tokens = ids_ref.shape
    per = heads // na
    rows = mb.shape[-2]
    slices = CLUSTERS // rows
    block = min(rows, LANES)
    blocks = rows // block
    width = per * HDIM
    height = w_ref.shape[0] // PIECES
    seq = lax.axis_index("seq")
    head = lax.axis_index("head")
    core = lax.rem(seq, CORES)
    chip = seq // CORES
    za = chip // nb
    xb = lax.rem(chip, nb)
    pool = na // heads_n
    half = za // pool
    spot = lax.rem(za, pool)
    sibling = {"seq": chip * CORES + 1 - core}

    def at_chip(target):
        return {"seq": target * CORES + core}

    def at_head(step):
        return {"head": lax.rem(head + step, heads_n)}

    def at_both(x, y):
        there = za * nb + lax.rem(xb + x, nb)
        return {"seq": there * CORES + core, "head": lax.rem(head + y, heads_n)}

    def at_mate(d, y):
        there = half * pool + lax.rem(spot + d, pool)
        return {"seq": (there * nb + xb) * CORES + core, "head": lax.rem(head + y, heads_n)}

    def remote(src, dst, send, recv, where):
        return pltpu.make_async_remote_copy(
            src_ref=src, dst_ref=dst, send_sem=send, recv_sem=recv, device_id=where, device_id_type=MESH
        )

    def chip_to(j):
        return lax.rem(chip + j, chips)

    def chip_from(j):
        return lax.rem(chip - j + chips, chips)

    def loads(g, number):
        src = (q_ref, k_ref, v_ref)[number]
        return pltpu.make_async_copy(
            src.at[:, pl.ds(pl.multiple_of(g * width, width), width)],
            qkv.at[number, g], load_sem.at[number, g],
        )

    for step in range(1, na + 1):
        loads(lax.rem(za + step, na), 0).start()

    barrier = pltpu.get_barrier_semaphore()
    targets = [sibling] + [at_chip(chip_to(j)) for j in range(1, chips)]
    targets += [at_head(step) for step in range(1, heads_n)]
    targets += [at_both(x, y) for x in range(1, nb) for y in range(1, heads_n)]
    targets += [at_mate(d, y) for d in range(1, pool) for y in range(1, heads_n)]
    for target in targets:
        pl.semaphore_signal(barrier, inc=1, device_id=target, device_id_type=MESH)

    own_ids = pltpu.make_async_copy(ids_ref, ids_all.at[spot, head], own_sem.at[1])
    own_ids.start()
    mine = half == head

    @pl.when(mine)
    def _():
        pltpu.make_async_copy(w_ref, wall.at[core, xb, head], own_sem.at[0]).start()

    @pl.when(jnp.logical_not(mine))
    def _():
        pltpu.make_async_copy(w_ref, line.at[half], own_sem.at[0]).start()

    for step in range(na):
        for number in (1, 2):
            loads(lax.rem(za + step, na), number).start()
    pl.semaphore_wait(barrier, len(targets))

    def span(p):
        return pl.ds(p * height, height)

    strides = na // pool

    def along(step, p, kept):
        there = lax.rem(za + step * pool, na) * nb + xb
        dst = wall.at[core, xb, head, span(p)] if kept else line.at[half, span(p)]
        return remote(
            w_ref.at[span(p)], dst, wz_send.at[step - 1, p], wz_recv.at[step - 1, p], at_chip(there)
        )

    def outward(x, y, p):
        group = lax.rem(head + y, heads_n)
        dst = wall.at[core, xb, head, span(p)]
        src = dst if y == 0 else line.at[group, span(p)]
        return remote(src, dst, wx_send.at[x, y, p], wx_recv.at[x, y, p], at_both(x, y))

    ways = [(x, y) for x in range(nb) for y in range(heads_n) if x or y]

    def over(p):
        part = wall.at[core, :, :, span(p)]
        return remote(part, part, wc_send.at[p], wc_recv.at[p], sibling)

    def stage_one(p):
        for kept in (True, False):

            @pl.when(mine if kept else jnp.logical_not(mine))
            def _(kept=kept):
                for step in range(1, strides):
                    along(step, p, kept).start()

    def stage_two(p):
        for step in range(1, strides):
            along(step, p, True).wait_recv()
        for x, y in ways:
            outward(x, y, p).start()

    def stage_three(p):
        for x, y in ways:
            outward(x, y, p).wait_recv()
        over(p).start()

    stages = (stage_one, stage_two, stage_three)

    end = PIECES + LAG * (len(stages) - 1)
    clock = [0]

    def tick():
        t = clock[0]
        if t >= end:
            return
        clock[0] = t + 1
        for number, stage in enumerate(stages):
            p = t - LAG * number
            if 0 <= p < PIECES:
                stage(p)

    def beat(name, at=0):
        counts = BEATS[name]
        for _ in range(counts[at] if at < len(counts) else 0):
            tick()

    def beats(name, k, first=0, count=na):
        for at in range(first, min(first + count, len(BEATS[name]))):
            if BEATS[name][at]:
                pl.when(k + first == at)(functools.partial(beat, name, at))

    tick()
    beat("start")
    id_copies = [
        remote(ids_ref, ids_all.at[spot, head], id_send.at[d, y], id_recv.at[d, y], at_mate(d, y))
        for d in range(pool)
        for y in range(heads_n)
        if d or y
    ]
    for copy in id_copies:
        copy.start()

    def exchange(phase, g):
        return [
            remote(
                outb.at[phase, g], recvb.at[phase, g],
                ex_send.at[phase, g, 0], ex_recv.at[phase, g, 0], sibling,
            ),
            remote(
                stat.at[phase, 1 - core, g], statr.at[phase, g],
                ex_send.at[phase, g, 1], ex_recv.at[phase, g, 1], sibling,
            ),
        ]

    def deliver(phase, j, number):
        target = chip_to(j)
        g, b = target // nb, lax.rem(target, nb)
        src, dst = ((mb, rx), (mc, rxc))[number]
        return remote(
            src.at[phase, g, b], dst.at[phase, j],
            rs_send.at[phase, j, number], rs_recv.at[phase, j, number], at_chip(target),
        )

    def hand_over(phase, g):
        for b in range(nb):
            outb[phase, g, b] = accf[1 - core, g, b].astype(BF16)
        for copy in exchange(phase, g):
            copy.start()

    def send_on(phase, g):
        for b in range(nb):
            j = lax.rem(g * nb + b - chip + chips, chips)

            @pl.when(j != 0)
            def _(j=j):
                for number in range(2):
                    deliver(phase, j, number).start()

    def places(i):
        for s in range(slices):
            number = i * slices + s
            yield slice(s * rows, (s + 1) * rows), number // CORES, number % CORES

    def tile_of(pieces):
        filled = [None] * STAT
        for at, column in pieces:
            for b in range(blocks):
                filled[at + b] = row_of(column[b * block : (b + 1) * block])
        blank = jnp.zeros((1, LANES), F32)
        return jnp.concatenate([blank if row is None else row for row in filled], axis=0)

    ones = jnp.ones((tokens, LANES), BF16)

    def merge_sums(g):
        for copy in exchange(0, g):
            copy.wait()
        for b in range(nb):
            total = accf[core, g, b] + recvb[0, g, b].astype(F32)
            accf[core, g, b] = total
            mb[0, g, b] = total.astype(BF16)
            mc[0, g, b] = stat[0, core, g, b] + statr[0, g, b]
        send_on(0, g)

    def sum_group(k, carry):
        g = lax.rem(za + 1 + k, na)
        loads(g, 0).wait()
        for i in range(per):
            member = one_hot(ids_ref[pl.ds(g * per + i, 1), :])
            both = jnp.concatenate([qkv[0, g, :, i * HDIM : (i + 1) * HDIM], ones], axis=1)
            result = jnp.dot(member, both, preferred_element_type=F32)
            for where, b, c in places(i):
                accf[c, g, b] = result[where, :HDIM]
                stat[0, c, g, b] = tile_of([(0, result[where, HDIM:])])
        hand_over(0, g)

        @pl.when(k == 0)
        def _():
            pltpu.make_async_copy(w_ref, line.at[half], own_sem.at[0]).wait()

        beats("sums", k)

        @pl.when(k > 0)
        def _():
            merge_sums(lax.rem(za + k, na))

        return carry

    lax.fori_loop(0, na, sum_group, 0)
    merge_sums(za)
    beat("owned")

    for j in range(1, chips):
        for number in range(2):
            deliver(0, j, number).wait()
        accf[core, za, xb] = accf[core, za, xb] + rx[0, j].astype(F32)
        mc[0, za, xb] = mc[0, za, xb] + rxc[0, j]
        beat("centre", j - 1)
    for b in range(blocks):
        where = slice(b * block, (b + 1) * block)
        count = columns_of(mc[0, za, xb, b : b + 1, :], block)
        full[chip, core, where, :] = (accf[core, za, xb, where, :] / count).astype(BF16)

    def spread(j):
        part = full.at[chip, core]
        return remote(part, part, ag_send.at[j], ag_recv.at[j], at_chip(chip_to(j)))

    def share(g):
        part = full.at[pl.ds(g * nb, nb), core]
        return remote(part, part, sib_send.at[g], sib_recv.at[g], sibling)

    def pass_group(g):
        for b in range(nb):
            j = lax.rem(chip - g * nb - b + chips, chips)

            @pl.when(j != 0)
            def _(j=j):
                spread(j).wait_recv()

        share(g).start()

    for k in range(na):
        for b in range(nb):
            j = lax.rem(lax.rem(za - k + na, na) * nb + b - chip + chips, chips)

            @pl.when(j != 0)
            def _(j=j):
                spread(j).start()

    beat("spread")
    pass_group(za)

    def merge_parts(g):
        for copy in exchange(1, g):
            copy.wait()
        for b in range(nb):
            left, right = stat[1, core, g, b], statr[1, g, b]
            peak = jnp.maximum(left[:MASS], right[:MASS])
            scale_l = jnp.exp2((left[:MASS] - peak) * SCALE)
            scale_r = jnp.exp2((right[:MASS] - peak) * SCALE)
            mass = left[MASS:] * scale_l + right[MASS:] * scale_r
            mc[1, g, b] = jnp.concatenate([peak, mass], axis=0)
            for x in range(blocks):
                where = slice(x * block, (x + 1) * block)
                total = accf[core, g, b, where, :] * columns_of(scale_l[x : x + 1], block)
                total += recvb[1, g, b, where, :].astype(F32) * columns_of(scale_r[x : x + 1], block)
                accf[core, g, b, where, :] = total
                mb[1, g, b, where, :] = total.astype(BF16)
        send_on(1, g)

    def attend_group(k, carry):
        g = lax.rem(za + k, na)
        following = lax.rem(g + 1, na)

        @pl.when((k >= 1) & (k + 1 < na))
        def _():
            pass_group(following)

        share(g).wait()
        loads(g, 1).wait()
        loads(g, 2).wait()
        for i in range(per):
            cols = slice(i * HDIM, (i + 1) * HDIM)
            centre = jnp.concatenate([full[g * nb + b, c] for _, b, c in places(i)], axis=0)
            scores = lax.dot_general(
                centre, qkv[1, g, :, cols], (((1,), (1,)), ((), ())), preferred_element_type=F32
            )
            peak = jnp.max(scores, axis=1, keepdims=True)
            weights = jnp.exp2((scores - peak) * SCALE).astype(BF16)
            both = jnp.concatenate([qkv[2, g, :, cols], ones], axis=1)
            result = jnp.dot(weights, both, preferred_element_type=F32)
            peak = jnp.broadcast_to(peak, (CLUSTERS, LANES))
            for where, b, c in places(i):
                accf[c, g, b] = result[where, :HDIM]
                stat[1, c, g, b] = tile_of([(0, peak[where]), (MASS, result[where, HDIM:])])
        hand_over(1, g)
        beats("attend", k)

        @pl.when(k == 0)
        def _():
            pass_group(following)

        @pl.when(k > 0)
        def _():
            merge_parts(lax.rem(g - 1 + na, na))

        return carry

    lax.fori_loop(0, na, attend_group, 0)
    beat("parts")
    merge_parts(lax.rem(za + na - 1, na))

    for j in range(1, chips):
        deliver(1, j, 1).wait()
    stats = [mc[1, za, xb]] + [rxc[1, j] for j in range(1, chips)]
    top = functools.reduce(jnp.maximum, [s[:MASS] for s in stats])
    scales = [jnp.exp2((s[:MASS] - top) * SCALE) for s in stats]
    mass = sum(s[MASS:] * scale for s, scale in zip(stats, scales))
    beat("stats")
    for j in range(chips):
        if j > 0:
            deliver(1, j, 0).wait()
        if j > 0:
            beat("merge", j - 1)
        for x in range(blocks):
            where = slice(x * block, (x + 1) * block)
            column = columns_of(scales[j][x : x + 1], block)
            if j == 0:
                accf[core, za, xb, where, :] = accf[core, za, xb, where, :] * column
            else:
                accf[core, za, xb, where, :] += rx[1, j, where, :].astype(F32) * column
    for x in range(blocks):
        where = slice(x * block, (x + 1) * block)
        total = columns_of(mass[x : x + 1], block)
        cev[head, chip, core, where, :] = (accf[core, za, xb, where, :] / total).astype(BF16)

    def spread_out(j):
        part = cev.at[head, chip, core]
        return remote(part, part, a2_send.at[j], a2_recv.at[j], at_chip(chip_to(j)))

    def cross(step, s):
        part = cev.at[head, s, core]
        return remote(part, part, y2_send.at[step - 1, s], y2_recv.at[step - 1, s], at_head(step))

    def share_out(h, s):
        part = cev.at[h, s, core]
        return remote(part, part, s2_send.at[h, s], s2_recv.at[h, s], sibling)

    for j in range(1, chips):
        spread_out(j).start()
    for step in range(1, heads_n):
        cross(step, chip).start()
    share_out(head, chip).start()
    beat("out")
    for j in range(1, chips):
        s = chip_from(j)
        spread_out(j).wait_recv()
        for step in range(1, heads_n):
            cross(step, s).start()
        share_out(head, s).start()
        beat("near", j - 1)
    for copy in id_copies:
        copy.wait()
    own_ids.wait()

    def gather(owner, first, beating, k, carry):
        h, g = lax.rem(head + first + k // na, heads_n), lax.rem(k, na)
        for i in range(per):
            member = one_hot(ids_all[owner, h, pl.ds(g * per + i, 1), :])
            centre = jnp.concatenate([cev[h, g * nb + b, c] for _, b, c in places(i)], axis=0)
            picked = lax.dot_general(member, centre, (((0,), (0,)), ((), ())), preferred_element_type=F32)
            qkv[h, g, :, i * HDIM : (i + 1) * HDIM] = picked.astype(BF16)
        if beating:
            beats("gather", k, first * na, na if first == 0 else (heads_n - 1) * na)
        return carry

    mate = lax.rem(spot + (1 if pool > 1 else 0), pool)

    def held(s, carry):
        share_out(head, s).wait()
        return carry

    lax.fori_loop(0, chips, held, 0)
    lax.fori_loop(0, na, functools.partial(gather, mate, 0, True), 0)
    for j in range(chips):
        s = chip_from(j)
        for step in range(1, heads_n):
            cross(step, s).wait_recv()
            share_out(lax.rem(head - step + heads_n, heads_n), s).start()
        beat("far", j)

    for j in range(1, chips):
        spread(j).wait_send()
        spread_out(j).wait_send()

    def settle(s, carry):
        for step in range(1, heads_n):
            share_out(lax.rem(head + step, heads_n), s).wait()
            cross(step, s).wait_send()
        return carry

    lax.fori_loop(0, chips, settle, 0)

    def project(b, c):
        total = None
        for h in range(heads_n):
            term = None
            for g in range(na):
                part = jnp.dot(
                    qkv[h, g], wall[c, b, h, g * width : (g + 1) * width, :],
                    preferred_element_type=F32,
                )
                term = part if term is None else term + part
            term = term.astype(BF16).astype(F32)
            total = term if total is None else total + term
        return total.astype(BF16)

    blocks_n = nb * CORES
    cols = w_ref.shape[1]

    def place_of(k):
        return pl.ds(pl.multiple_of((spot * blocks_n + k) * cols, cols), cols)

    def give(d, k):
        return remote(
            outbox.at[d - 1, k], out_ref.at[:, place_of(k)],
            out_send.at[d - 1, k], out_recv.at[d - 1, k], at_mate(d, 0),
        )

    for d in [*range(1, pool), 0]:
        owner = lax.rem(spot + d, pool)
        leading = d == (1 if pool > 1 else 0)
        first = 1 if leading else 0
        lax.fori_loop(0, (heads_n - first) * na, functools.partial(gather, owner, first, leading), 0)
        if leading:
            while clock[0] < end:
                tick()

            def landed(p, carry):
                over(p).wait_recv()
                return carry

            lax.fori_loop(0, PIECES, landed, 0)

        def column(k, carry, d=d):
            result = project(k // CORES, lax.rem(k, CORES))
            if d == 0:
                out_ref[:, place_of(k)] = result
            else:
                outbox[d - 1, k] = result
                give(d, k).start()
            return carry

        lax.fori_loop(0, blocks_n, column, 0)

    for d in range(1, pool):
        for k in range(blocks_n):
            give(d, k).wait()

    def finish(p, carry):
        for step in range(1, strides):
            along(step, p, True).wait_send()
        for x, y in ways:
            outward(x, y, p).wait_send()
        over(p).wait_send()
        return carry

    lax.fori_loop(0, PIECES, finish, 0)


def local(queries, keys, values, cluster_ids, out_weight):
    n = lax.axis_size("seq")
    heads_n = lax.axis_size("head")
    chips, na, nb = grid_of(n)
    tokens = queries.shape[0]
    heads = queries.shape[1] // HDIM
    rows = heads * CLUSTERS // n
    width = heads // na * HDIM
    depth, cols = out_weight.shape
    pool = na // heads_n
    ids_t = cluster_ids.T

    vmem = pl.BlockSpec(memory_space=pltpu.VMEM)
    anywhere = pl.BlockSpec(memory_space=pl.ANY)
    dma = pltpu.SemaphoreType.DMA

    def pair(*shape):
        shape = tuple(max(size, 1) for size in shape)
        return [dma(shape), dma(shape)]

    blocks_n = CORES * nb
    return pl.pallas_call(
        functools.partial(fused_kernel, n, heads_n),
        out_shape=jax.ShapeDtypeStruct((tokens, blocks_n * pool * cols), BF16),
        in_specs=[vmem, anywhere, anywhere, anywhere, anywhere],
        out_specs=vmem,
        scratch_shapes=[
            pltpu.VMEM((heads_n, chips, CORES, rows, HDIM), BF16),
            pltpu.VMEM((CORES, nb, heads_n, depth, cols), BF16),
            pltpu.VMEM((pool, heads_n, heads, tokens), jnp.int32),
            pltpu.VMEM((max(pool - 1, 1), blocks_n, tokens, cols), BF16),
            pltpu.VMEM((max(3, heads_n), na, tokens, width), BF16),
            pltpu.VMEM((heads_n, depth, cols), BF16),
            pltpu.VMEM((CORES, na, nb, rows, HDIM), F32),
            pltpu.VMEM((2, CORES, na, nb, STAT, LANES), F32),
            pltpu.VMEM((2, na, nb, rows, HDIM), BF16),
            pltpu.VMEM((2, na, nb, rows, HDIM), BF16),
            pltpu.VMEM((2, na, nb, STAT, LANES), F32),
            pltpu.VMEM((2, na, nb, rows, HDIM), BF16),
            pltpu.VMEM((2, na, nb, STAT, LANES), F32),
            pltpu.VMEM((2, chips, rows, HDIM), BF16),
            pltpu.VMEM((2, chips, STAT, LANES), F32),
            pltpu.VMEM((chips, CORES, rows, HDIM), BF16),
            dma((3, na)), dma((2,)),
            *pair(pool, heads_n),
            *pair(2, na, 2), *pair(2, chips, 2), *pair(chips), *pair(na),
            *pair(chips), *pair(heads_n - 1, chips), *pair(heads_n, chips),
            *pair(na // pool - 1, PIECES), *pair(nb, heads_n, PIECES), *pair(PIECES),
            *pair(pool - 1, blocks_n),
        ],
        compiler_params=pltpu.CompilerParams(
            collective_id=0, has_side_effects=True, vmem_limit_bytes=60 << 20
        ),
    )(ids_t, queries, keys, values, out_weight)


def solution(mesh):
    return jax.shard_map(
        local,
        mesh=mesh,
        in_specs=(
            P("seq", "head"),
            P("seq", "head"),
            P("seq", "head"),
            P("seq", "head"),
            P("head", "seq"),
        ),
        out_specs=P("seq", "head"),
        check_vma=False,
    )
```

```python
import functools
import math

import jax
import jax.numpy as jnp
from jax import lax
from jax.experimental import pallas as pl
from jax.experimental.pallas import tpu as pltpu
from jax.sharding import PartitionSpec as P

HDIM = 128
CLUSTERS = 256
LANES = 128
STAT = 8
MASS = 4
CORES = 2
PIECES = 16
LAG = 2
BEATS = {'start': (), 'sums': (0, 1, 0, 1), 'owned': (1,), 'centre': (), 'spread': (2,), 'attend': (1, 1, 1, 1), 'parts': (1,), 'stats': (1,), 'merge': (), 'out': (2,), 'near': (0, 0, 0, 0), 'far': (), 'gather': (1, 1, 1, 1, 1, 1, 1)}
MESH = pl.DeviceIdType.MESH
F32 = jnp.float32
BF16 = jnp.bfloat16
SCALE = math.log2(math.e) / math.sqrt(HDIM)


def grid_of(n):
    chips = n // CORES
    bits = chips.bit_length() - 1
    a = 1 << ((bits + 1) // 2)
    return chips, a, chips // a


def columns_of(row, block):
    return jnp.broadcast_to(row, (LANES, LANES)).T[:block]


def row_of(column):
    block = column.shape[0]
    return jnp.concatenate([column] * (LANES // block), axis=0).T[:1]


def one_hot(ids_row):
    labels = lax.broadcasted_iota(jnp.int32, (CLUSTERS, ids_row.shape[1]), 0).astype(BF16)
    return jnp.where(labels == ids_row.astype(BF16), jnp.ones((), BF16), jnp.zeros((), BF16))


def fused_kernel(
    n, heads_n, ids_ref, q_ref, k_ref, v_ref, w_ref, out_ref,
    cev, wall, ids_all, outbox, qkv, line, accf, stat, outb, recvb, statr, mb, mc, rxx, rxxc, rx, rxc, full,
    load_sem, own_sem, id_send, id_recv, ex_send, ex_recv, sd_send, sd_recv, rs_send, rs_recv, ag_send, ag_recv,
    sib_send, sib_recv, a2_send, a2_recv, hx_send, hx_recv, h2_send, h2_recv, y2_send, y2_recv, s2_send, s2_recv,
    wz_send, wz_recv, wx_send, wx_recv, wc_send, wc_recv, out_send, out_recv,
):
    chips, na, nb = grid_of(n)
    heads, tokens = ids_ref.shape
    per = heads // na
    rows = mb.shape[-2]
    slices = CLUSTERS // rows
    block = min(rows, LANES)
    blocks = rows // block
    width = per * HDIM
    height = w_ref.shape[0] // PIECES
    seq = lax.axis_index("seq")
    head = lax.axis_index("head")
    core = lax.rem(seq, CORES)
    chip = seq // CORES
    za = chip // nb
    xb = lax.rem(chip, nb)
    pool = na // heads_n
    half = za // pool
    spot = lax.rem(za, pool)
    sibling = {"seq": chip * CORES + 1 - core}

    def at_chip(target):
        return {"seq": target * CORES + core}

    def at_head(step):
        return {"head": lax.rem(head + step, heads_n)}

    def at_both(x, y):
        there = za * nb + lax.rem(xb + x, nb)
        return {"seq": there * CORES + core, "head": lax.rem(head + y, heads_n)}

    def at_mate(d, y):
        there = half * pool + lax.rem(spot + d, pool)
        return {"seq": (there * nb + xb) * CORES + core, "head": lax.rem(head + y, heads_n)}

    def remote(src, dst, send, recv, where):
        return pltpu.make_async_remote_copy(
            src_ref=src, dst_ref=dst, send_sem=send, recv_sem=recv, device_id=where, device_id_type=MESH
        )

    def chip_from(j):
        return lax.rem(chip - j + chips, chips)

    def loads(g, number):
        src = (q_ref, k_ref, v_ref)[number]
        return pltpu.make_async_copy(
            src.at[:, pl.ds(pl.multiple_of(g * width, width), width)],
            qkv.at[number, g], load_sem.at[number, g],
        )

    for step in range(1, na + 1):
        loads(lax.rem(za + step, na), 0).start()

    barrier = pltpu.get_barrier_semaphore()
    targets = [sibling]
    targets += [at_chip(lax.rem(za + step, na) * nb + xb) for step in range(1, na)]
    targets += [at_chip(za * nb + lax.rem(xb + step, nb)) for step in range(1, nb)]
    targets += [at_head(step) for step in range(1, heads_n)]
    targets += [at_both(x, y) for x in range(1, nb) for y in range(1, heads_n)]
    targets += [at_mate(d, y) for d in range(1, pool) for y in range(1, heads_n)]
    for target in targets:
        pl.semaphore_signal(barrier, inc=1, device_id=target, device_id_type=MESH)

    own_ids = pltpu.make_async_copy(ids_ref, ids_all.at[spot, head], own_sem.at[1])
    own_ids.start()
    mine = half == head

    @pl.when(mine)
    def _():
        pltpu.make_async_copy(w_ref, wall.at[core, xb, head], own_sem.at[0]).start()

    @pl.when(jnp.logical_not(mine))
    def _():
        pltpu.make_async_copy(w_ref, line.at[half], own_sem.at[0]).start()

    for step in range(na):
        for number in (1, 2):
            loads(lax.rem(za + step, na), number).start()
    pl.semaphore_wait(barrier, len(targets))

    def span(p):
        return pl.ds(p * height, height)

    strides = na // pool

    def along(step, p, kept):
        there = lax.rem(za + step * pool, na) * nb + xb
        dst = wall.at[core, xb, head, span(p)] if kept else line.at[half, span(p)]
        return remote(
            w_ref.at[span(p)], dst, wz_send.at[step - 1, p], wz_recv.at[step - 1, p], at_chip(there)
        )

    def outward(x, y, p):
        group = lax.rem(head + y, heads_n)
        dst = wall.at[core, xb, head, span(p)]
        src = dst if y == 0 else line.at[group, span(p)]
        return remote(src, dst, wx_send.at[x, y, p], wx_recv.at[x, y, p], at_both(x, y))

    ways = [(x, y) for x in range(nb) for y in range(heads_n) if x or y]

    def over(p):
        part = wall.at[core, :, :, span(p)]
        return remote(part, part, wc_send.at[p], wc_recv.at[p], sibling)

    def stage_one(p):
        for kept in (True, False):

            @pl.when(mine if kept else jnp.logical_not(mine))
            def _(kept=kept):
                for step in range(1, strides):
                    along(step, p, kept).start()

    def stage_two(p):
        for step in range(1, strides):
            along(step, p, True).wait_recv()
        for x, y in ways:
            outward(x, y, p).start()

    def stage_three(p):
        for x, y in ways:
            outward(x, y, p).wait_recv()
        over(p).start()

    stages = (stage_one, stage_two, stage_three)

    end = PIECES + LAG * (len(stages) - 1)
    clock = [0]

    def tick():
        t = clock[0]
        if t >= end:
            return
        clock[0] = t + 1
        for number, stage in enumerate(stages):
            p = t - LAG * number
            if 0 <= p < PIECES:
                stage(p)

    def beat(name, at=0):
        counts = BEATS[name]
        for _ in range(counts[at] if at < len(counts) else 0):
            tick()

    def beats(name, k, first=0, count=na):
        for at in range(first, min(first + count, len(BEATS[name]))):
            if BEATS[name][at]:
                pl.when(k + first == at)(functools.partial(beat, name, at))

    tick()
    beat("start")
    id_copies = [
        remote(ids_ref, ids_all.at[spot, head], id_send.at[d, y], id_recv.at[d, y], at_mate(d, y))
        for d in range(pool)
        for y in range(heads_n)
        if d or y
    ]
    for copy in id_copies:
        copy.start()

    def exchange(phase, g):
        return [
            remote(
                outb.at[phase, g], recvb.at[phase, g],
                ex_send.at[phase, g, 0], ex_recv.at[phase, g, 0], sibling,
            ),
            remote(
                stat.at[phase, 1 - core, g], statr.at[phase, g],
                ex_send.at[phase, g, 1], ex_recv.at[phase, g, 1], sibling,
            ),
        ]

    def side(phase, g, step, number):
        b = lax.rem(xb + step, nb)
        src, dst = ((mb, rxx), (mc, rxxc))[number]
        return remote(
            src.at[phase, g, b], dst.at[phase, g, step],
            sd_send.at[phase, g, step, number], sd_recv.at[phase, g, step, number], at_chip(za * nb + b),
        )

    def deliver(phase, step, number):
        g = lax.rem(za + step, na)
        src, dst = ((mb, rx), (mc, rxc))[number]
        return remote(
            src.at[phase, g, xb], dst.at[phase, step],
            rs_send.at[phase, step, number], rs_recv.at[phase, step, number], at_chip(g * nb + xb),
        )

    def hand_over(phase, g):
        for b in range(nb):
            outb[phase, g, b] = accf[1 - core, g, b].astype(BF16)
        for copy in exchange(phase, g):
            copy.start()

    def send_side(phase, g):
        for step in range(1, nb):
            for number in range(2):
                side(phase, g, step, number).start()

    def wait_side(phase, g):
        for step in range(1, nb):
            for number in range(2):
                side(phase, g, step, number).wait()

    def send_on(phase, g):
        mb[phase, g, xb] = accf[core, g, xb].astype(BF16)
        step = lax.rem(g - za + na, na)

        @pl.when(step != 0)
        def _():
            for number in range(2):
                deliver(phase, step, number).start()

    def places(i):
        for s in range(slices):
            number = i * slices + s
            yield slice(s * rows, (s + 1) * rows), number // CORES, number % CORES

    def tile_of(pieces):
        filled = [None] * STAT
        for at, column in pieces:
            for b in range(blocks):
                filled[at + b] = row_of(column[b * block : (b + 1) * block])
        blank = jnp.zeros((1, LANES), F32)
        return jnp.concatenate([blank if row is None else row for row in filled], axis=0)

    ones = jnp.ones((tokens, LANES), BF16)

    def merge_sums(g):
        for copy in exchange(0, g):
            copy.wait()
        for b in range(nb):
            total = accf[core, g, b] + recvb[0, g, b].astype(F32)
            accf[core, g, b] = total
            mb[0, g, b] = total.astype(BF16)
            mc[0, g, b] = stat[0, core, g, b] + statr[0, g, b]
        send_side(0, g)

    def merge_side_sums(g):
        wait_side(0, g)
        for step in range(1, nb):
            accf[core, g, xb] = accf[core, g, xb] + rxx[0, g, step].astype(F32)
            mc[0, g, xb] = mc[0, g, xb] + rxxc[0, g, step]
        send_on(0, g)

    def sum_group(k, carry):
        g = lax.rem(za + 1 + k, na)
        loads(g, 0).wait()
        for i in range(per):
            member = one_hot(ids_ref[pl.ds(g * per + i, 1), :])
            both = jnp.concatenate([qkv[0, g, :, i * HDIM : (i + 1) * HDIM], ones], axis=1)
            result = jnp.dot(member, both, preferred_element_type=F32)
            for where, b, c in places(i):
                accf[c, g, b] = result[where, :HDIM]
                stat[0, c, g, b] = tile_of([(0, result[where, HDIM:])])
        hand_over(0, g)

        @pl.when(k == 0)
        def _():
            pltpu.make_async_copy(w_ref, line.at[half], own_sem.at[0]).wait()

        beats("sums", k)

        @pl.when(k > 0)
        def _():
            merge_sums(lax.rem(za + k, na))

        @pl.when(k > 1)
        def _():
            merge_side_sums(lax.rem(za + k - 1, na))

        return carry

    lax.fori_loop(0, na, sum_group, 0)
    merge_sums(za)
    merge_side_sums(lax.rem(za + na - 1, na))
    beat("owned")
    merge_side_sums(za)

    for j in range(1, na):
        for number in range(2):
            deliver(0, j, number).wait()
        accf[core, za, xb] = accf[core, za, xb] + rx[0, j].astype(F32)
        mc[0, za, xb] = mc[0, za, xb] + rxc[0, j]
        beat("centre", j - 1)
    for b in range(blocks):
        where = slice(b * block, (b + 1) * block)
        count = columns_of(mc[0, za, xb, b : b + 1, :], block)
        full[chip, core, where, :] = (accf[core, za, xb, where, :] / count).astype(BF16)

    def spread(step):
        part = full.at[chip, core]
        there = lax.rem(za + na - step, na) * nb + xb
        return remote(part, part, ag_send.at[step], ag_recv.at[step], at_chip(there))

    def hop(step, g):
        part = full.at[g * nb + xb, core]
        there = za * nb + lax.rem(xb + step, nb)
        return remote(part, part, hx_send.at[step, g], hx_recv.at[step, g], at_chip(there))

    def share(g):
        part = full.at[pl.ds(g * nb, nb), core]
        return remote(part, part, sib_send.at[g], sib_recv.at[g], sibling)

    def share_group(g):
        for step in range(1, nb):
            hop(step, g).wait_recv()
        share(g).start()

    for step in range(1, nb):
        hop(step, za).start()
    for step in range(1, na):
        spread(step).start()
    beat("spread")
    share_group(za)

    def combine(g, b, left, right, part):
        peak = jnp.maximum(left[:MASS], right[:MASS])
        scale_l = jnp.exp2((left[:MASS] - peak) * SCALE)
        scale_r = jnp.exp2((right[:MASS] - peak) * SCALE)
        mass = left[MASS:] * scale_l + right[MASS:] * scale_r
        mc[1, g, b] = jnp.concatenate([peak, mass], axis=0)
        for x in range(blocks):
            where = slice(x * block, (x + 1) * block)
            total = accf[core, g, b, where, :] * columns_of(scale_l[x : x + 1], block)
            total += part[where].astype(F32) * columns_of(scale_r[x : x + 1], block)
            accf[core, g, b, where, :] = total

    def merge_parts(g):
        for copy in exchange(1, g):
            copy.wait()
        for b in range(nb):
            combine(g, b, stat[1, core, g, b], statr[1, g, b], recvb[1, g, b])
            mb[1, g, b] = accf[core, g, b].astype(BF16)
        send_side(1, g)

    def merge_side_parts(g):
        wait_side(1, g)
        for step in range(1, nb):
            combine(g, xb, mc[1, g, xb], rxxc[1, g, step], rxx[1, g, step])
        send_on(1, g)

    def attend_group(k, carry):
        g = lax.rem(za + k, na)
        following = lax.rem(g + 1, na)

        @pl.when(k + 1 < na)
        def _():
            spread(k + 1).wait_recv()
            for step in range(1, nb):
                hop(step, following).start()

        share(g).wait()
        loads(g, 1).wait()
        loads(g, 2).wait()
        for i in range(per):
            cols = slice(i * HDIM, (i + 1) * HDIM)
            centre = jnp.concatenate([full[g * nb + b, c] for _, b, c in places(i)], axis=0)
            scores = lax.dot_general(
                centre, qkv[1, g, :, cols], (((1,), (1,)), ((), ())), preferred_element_type=F32
            )
            peak = jnp.max(scores, axis=1, keepdims=True)
            weights = jnp.exp2((scores - peak) * SCALE).astype(BF16)
            both = jnp.concatenate([qkv[2, g, :, cols], ones], axis=1)
            result = jnp.dot(weights, both, preferred_element_type=F32)
            peak = jnp.broadcast_to(peak, (CLUSTERS, LANES))
            for where, b, c in places(i):
                accf[c, g, b] = result[where, :HDIM]
                stat[1, c, g, b] = tile_of([(0, peak[where]), (MASS, result[where, HDIM:])])
        hand_over(1, g)
        beats("attend", k)

        @pl.when(k + 1 < na)
        def _():
            share_group(following)

        @pl.when(k > 0)
        def _():
            merge_parts(lax.rem(g - 1 + na, na))

        @pl.when(k > 1)
        def _():
            merge_side_parts(lax.rem(g - 2 + na, na))

        return carry

    lax.fori_loop(0, na, attend_group, 0)
    beat("parts")
    merge_parts(lax.rem(za + na - 1, na))
    if na > 1:
        merge_side_parts(lax.rem(za + na - 2, na))
    merge_side_parts(lax.rem(za + na - 1, na))

    for j in range(1, na):
        deliver(1, j, 1).wait()
    stats = [mc[1, za, xb]] + [rxc[1, j] for j in range(1, na)]
    top = functools.reduce(jnp.maximum, [s[:MASS] for s in stats])
    scales = [jnp.exp2((s[:MASS] - top) * SCALE) for s in stats]
    mass = sum(s[MASS:] * scale for s, scale in zip(stats, scales))
    beat("stats")
    for j in range(na):
        if j > 0:
            deliver(1, j, 0).wait()
        if j > 0:
            beat("merge", j - 1)
        for x in range(blocks):
            where = slice(x * block, (x + 1) * block)
            column = columns_of(scales[j][x : x + 1], block)
            if j == 0:
                accf[core, za, xb, where, :] = accf[core, za, xb, where, :] * column
            else:
                accf[core, za, xb, where, :] += rx[1, j, where, :].astype(F32) * column
    for x in range(blocks):
        where = slice(x * block, (x + 1) * block)
        total = columns_of(mass[x : x + 1], block)
        cev[head, chip, core, where, :] = (accf[core, za, xb, where, :] / total).astype(BF16)

    def spread_out(step):
        part = cev.at[head, chip, core]
        there = lax.rem(za + na - step, na) * nb + xb
        return remote(part, part, a2_send.at[step], a2_recv.at[step], at_chip(there))

    def hop_out(step, g):
        part = cev.at[head, g * nb + xb, core]
        there = za * nb + lax.rem(xb + step, nb)
        return remote(part, part, h2_send.at[step, g], h2_recv.at[step, g], at_chip(there))

    def cross(step, s):
        part = cev.at[head, s, core]
        return remote(part, part, y2_send.at[step - 1, s], y2_recv.at[step - 1, s], at_head(step))

    def share_out(h, s):
        part = cev.at[h, s, core]
        return remote(part, part, s2_send.at[h, s], s2_recv.at[h, s], sibling)

    def pass_on(s):
        for step in range(1, heads_n):
            cross(step, s).start()
        share_out(head, s).start()

    for step in range(1, na):
        spread_out(step).start()
    for step in range(1, nb):
        hop_out(step, za).start()
    pass_on(chip)
    beat("out")
    for k in range(na):
        g = lax.rem(za + k, na)
        if k + 1 < na:
            spread_out(k + 1).wait_recv()
            following = lax.rem(za + k + 1, na)
            for step in range(1, nb):
                hop_out(step, following).start()
            pass_on(following * nb + xb)
        for step in range(1, nb):
            hop_out(step, g).wait_recv()
            pass_on(g * nb + lax.rem(xb - step + nb, nb))
        beat("near", k)

    for copy in id_copies:
        copy.wait()
    own_ids.wait()

    def gather(owner, first, beating, k, carry):
        h, g = lax.rem(head + first + k // na, heads_n), lax.rem(k, na)
        for i in range(per):
            member = one_hot(ids_all[owner, h, pl.ds(g * per + i, 1), :])
            centre = jnp.concatenate([cev[h, g * nb + b, c] for _, b, c in places(i)], axis=0)
            picked = lax.dot_general(member, centre, (((0,), (0,)), ((), ())), preferred_element_type=F32)
            qkv[h, g, :, i * HDIM : (i + 1) * HDIM] = picked.astype(BF16)
        if beating:
            beats("gather", k, first * na, na if first == 0 else (heads_n - 1) * na)
        return carry

    mate = lax.rem(spot + (1 if pool > 1 else 0), pool)

    def held(s, carry):
        share_out(head, s).wait()
        return carry

    lax.fori_loop(0, chips, held, 0)
    lax.fori_loop(0, na, functools.partial(gather, mate, 0, True), 0)
    for j in range(chips):
        s = chip_from(j)
        for step in range(1, heads_n):
            cross(step, s).wait_recv()
            share_out(lax.rem(head - step + heads_n, heads_n), s).start()
        beat("far", j)

    for step in range(1, na):
        spread(step).wait_send()
        spread_out(step).wait_send()
    for g in range(na):
        for step in range(1, nb):
            hop(step, g).wait_send()
            hop_out(step, g).wait_send()

    def settle(s, carry):
        for step in range(1, heads_n):
            share_out(lax.rem(head + step, heads_n), s).wait()
            cross(step, s).wait_send()
        return carry

    lax.fori_loop(0, chips, settle, 0)

    def project(b, c):
        total = None
        for h in range(heads_n):
            term = None
            for g in range(na):
                part = jnp.dot(
                    qkv[h, g], wall[c, b, h, g * width : (g + 1) * width, :],
                    preferred_element_type=F32,
                )
                term = part if term is None else term + part
            term = term.astype(BF16).astype(F32)
            total = term if total is None else total + term
        return total.astype(BF16)

    blocks_n = nb * CORES
    cols = w_ref.shape[1]

    def place_of(k):
        return pl.ds(pl.multiple_of((spot * blocks_n + k) * cols, cols), cols)

    def give(d, k):
        return remote(
            outbox.at[d - 1, k], out_ref.at[:, place_of(k)],
            out_send.at[d - 1, k], out_recv.at[d - 1, k], at_mate(d, 0),
        )

    for d in [*range(1, pool), 0]:
        owner = lax.rem(spot + d, pool)
        leading = d == (1 if pool > 1 else 0)
        first = 1 if leading else 0
        lax.fori_loop(0, (heads_n - first) * na, functools.partial(gather, owner, first, leading), 0)
        if leading:
            while clock[0] < end:
                tick()

            def landed(p, carry):
                over(p).wait_recv()
                return carry

            lax.fori_loop(0, PIECES, landed, 0)

        def column(k, carry, d=d):
            result = project(k // CORES, lax.rem(k, CORES))
            if d == 0:
                out_ref[:, place_of(k)] = result
            else:
                outbox[d - 1, k] = result
                give(d, k).start()
            return carry

        lax.fori_loop(0, blocks_n, column, 0)

    for d in range(1, pool):
        for k in range(blocks_n):
            give(d, k).wait()

    def finish(p, carry):
        for step in range(1, strides):
            along(step, p, True).wait_send()
        for x, y in ways:
            outward(x, y, p).wait_send()
        over(p).wait_send()
        return carry

    lax.fori_loop(0, PIECES, finish, 0)


def local(queries, keys, values, cluster_ids, out_weight):
    n = lax.axis_size("seq")
    heads_n = lax.axis_size("head")
    chips, na, nb = grid_of(n)
    tokens = queries.shape[0]
    heads = queries.shape[1] // HDIM
    rows = heads * CLUSTERS // n
    width = heads // na * HDIM
    depth, cols = out_weight.shape
    pool = na // heads_n
    ids_t = cluster_ids.T

    vmem = pl.BlockSpec(memory_space=pltpu.VMEM)
    anywhere = pl.BlockSpec(memory_space=pl.ANY)
    dma = pltpu.SemaphoreType.DMA

    def pair(*shape):
        shape = tuple(max(size, 1) for size in shape)
        return [dma(shape), dma(shape)]

    blocks_n = CORES * nb
    return pl.pallas_call(
        functools.partial(fused_kernel, n, heads_n),
        out_shape=jax.ShapeDtypeStruct((tokens, blocks_n * pool * cols), BF16),
        in_specs=[vmem, anywhere, anywhere, anywhere, anywhere],
        out_specs=vmem,
        scratch_shapes=[
            pltpu.VMEM((heads_n, chips, CORES, rows, HDIM), BF16),
            pltpu.VMEM((CORES, nb, heads_n, depth, cols), BF16),
            pltpu.VMEM((pool, heads_n, heads, tokens), jnp.int32),
            pltpu.VMEM((max(pool - 1, 1), blocks_n, tokens, cols), BF16),
            pltpu.VMEM((max(3, heads_n), na, tokens, width), BF16),
            pltpu.VMEM((heads_n, depth, cols), BF16),
            pltpu.VMEM((CORES, na, nb, rows, HDIM), F32),
            pltpu.VMEM((2, CORES, na, nb, STAT, LANES), F32),
            pltpu.VMEM((2, na, nb, rows, HDIM), BF16),
            pltpu.VMEM((2, na, nb, rows, HDIM), BF16),
            pltpu.VMEM((2, na, nb, STAT, LANES), F32),
            pltpu.VMEM((2, na, nb, rows, HDIM), BF16),
            pltpu.VMEM((2, na, nb, STAT, LANES), F32),
            pltpu.VMEM((2, na, nb, rows, HDIM), BF16),
            pltpu.VMEM((2, na, nb, STAT, LANES), F32),
            pltpu.VMEM((2, na, rows, HDIM), BF16),
            pltpu.VMEM((2, na, STAT, LANES), F32),
            pltpu.VMEM((chips, CORES, rows, HDIM), BF16),
            dma((3, na)), dma((2,)),
            *pair(pool, heads_n),
            *pair(2, na, 2), *pair(2, na, nb, 2), *pair(2, na, 2), *pair(chips), *pair(na),
            *pair(chips), *pair(nb, na), *pair(nb, na),
            *pair(heads_n - 1, chips), *pair(heads_n, chips),
            *pair(na // pool - 1, PIECES), *pair(nb, heads_n, PIECES), *pair(PIECES),
            *pair(pool - 1, blocks_n),
        ],
        compiler_params=pltpu.CompilerParams(
            collective_id=0, has_side_effects=True, vmem_limit_bytes=60 << 20
        ),
    )(ids_t, queries, keys, values, out_weight)


def solution(mesh):
    return jax.shard_map(
        local,
        mesh=mesh,
        in_specs=(
            P("seq", "head"),
            P("seq", "head"),
            P("seq", "head"),
            P("seq", "head"),
            P("head", "seq"),
        ),
        out_specs=P("seq", "head"),
        check_vma=False,
    )
```

```python
import functools
import math

import jax
import jax.numpy as jnp
from jax import lax
from jax.experimental import pallas as pl
from jax.experimental.pallas import tpu as pltpu
from jax.sharding import PartitionSpec as P

HDIM = 128
CLUSTERS = 256
LANES = 128
STAT = 8
MASS = 4
CORES = 2
PIECES = 16
LAG = 2
BEATS = {'start': (), 'sums': (0, 1, 0, 1), 'owned': (1,), 'centre': (), 'spread': (2,), 'attend': (1, 1, 1, 1), 'parts': (1,), 'stats': (1,), 'merge': (), 'out': (2,), 'near': (0, 0, 0, 0), 'far': (), 'gather': (1, 1, 1, 1, 1, 1, 1)}
MESH = pl.DeviceIdType.MESH
F32 = jnp.float32
BF16 = jnp.bfloat16
SCALE = math.log2(math.e) / math.sqrt(HDIM)


def grid_of(n):
    chips = n // CORES
    bits = chips.bit_length() - 1
    a = 1 << ((bits + 1) // 2)
    return chips, a, chips // a


def columns_of(row, block):
    return jnp.broadcast_to(row, (LANES, LANES)).T[:block]


def row_of(column):
    block = column.shape[0]
    return jnp.concatenate([column] * (LANES // block), axis=0).T[:1]


def one_hot(ids_row):
    labels = lax.broadcasted_iota(jnp.int32, (CLUSTERS, ids_row.shape[1]), 0).astype(BF16)
    return jnp.where(labels == ids_row.astype(BF16), jnp.ones((), BF16), jnp.zeros((), BF16))


def fused_kernel(
    n, heads_n, ids_ref, q_ref, k_ref, v_ref, w_ref, out_ref,
    cev, wall, ids_all, outbox, qkv, line, accf, stat, outb, recvb, statr, mb, mc, rxx, rxxc, rx, rxc, full,
    load_sem, own_sem, id_send, id_recv, ex_send, ex_recv, sd_send, sd_recv, rs_send, rs_recv, ag_send, ag_recv,
    sib_send, sib_recv, a2_send, a2_recv, hx_send, hx_recv, h2_send, h2_recv, y2_send, y2_recv, s2_send, s2_recv,
    wz_send, wz_recv, wx_send, wx_recv, wc_send, wc_recv, out_send, out_recv,
):
    chips, na, nb = grid_of(n)
    heads, tokens = ids_ref.shape
    per = heads // na
    rows = mb.shape[-2]
    slices = CLUSTERS // rows
    block = min(rows, LANES)
    blocks = rows // block
    width = per * HDIM
    height = w_ref.shape[0] // PIECES
    seq = lax.axis_index("seq")
    head = lax.axis_index("head")
    core = lax.rem(seq, CORES)
    chip = seq // CORES
    za = chip // nb
    xb = lax.rem(chip, nb)
    pool = na // heads_n
    half = za // pool
    spot = lax.rem(za, pool)
    sibling = {"seq": chip * CORES + 1 - core}

    def at_chip(target):
        return {"seq": target * CORES + core}

    def at_head(step):
        return {"head": lax.rem(head + step, heads_n)}

    def at_both(x, y):
        there = za * nb + lax.rem(xb + x, nb)
        return {"seq": there * CORES + core, "head": lax.rem(head + y, heads_n)}

    def at_mate(d, y):
        there = half * pool + lax.rem(spot + d, pool)
        return {"seq": (there * nb + xb) * CORES + core, "head": lax.rem(head + y, heads_n)}

    def remote(src, dst, send, recv, where):
        return pltpu.make_async_remote_copy(
            src_ref=src, dst_ref=dst, send_sem=send, recv_sem=recv, device_id=where, device_id_type=MESH
        )

    def chip_from(j):
        return lax.rem(chip - j + chips, chips)

    def loads(g, number):
        src = (q_ref, k_ref, v_ref)[number]
        return pltpu.make_async_copy(
            src.at[:, pl.ds(pl.multiple_of(g * width, width), width)],
            qkv.at[number, g], load_sem.at[number, g],
        )

    for step in range(1, na + 1):
        loads(lax.rem(za + step, na), 0).start()

    barrier = pltpu.get_barrier_semaphore()
    targets = [sibling]
    targets += [at_chip(lax.rem(za + step, na) * nb + xb) for step in range(1, na)]
    targets += [at_chip(za * nb + lax.rem(xb + step, nb)) for step in range(1, nb)]
    targets += [at_head(step) for step in range(1, heads_n)]
    targets += [at_both(x, y) for x in range(1, nb) for y in range(1, heads_n)]
    targets += [at_mate(d, y) for d in range(1, pool) for y in range(1, heads_n)]
    for target in targets:
        pl.semaphore_signal(barrier, inc=1, device_id=target, device_id_type=MESH)

    own_ids = pltpu.make_async_copy(ids_ref, ids_all.at[spot, head], own_sem.at[1])
    own_ids.start()
    mine = half == head

    @pl.when(mine)
    def _():
        pltpu.make_async_copy(w_ref, wall.at[core, xb, head], own_sem.at[0]).start()

    @pl.when(jnp.logical_not(mine))
    def _():
        pltpu.make_async_copy(w_ref, line.at[half], own_sem.at[0]).start()

    for step in range(na):
        for number in (1, 2):
            loads(lax.rem(za + step, na), number).start()
    pl.semaphore_wait(barrier, len(targets))

    def span(p):
        return pl.ds(p * height, height)

    strides = na // pool

    def along(step, p, kept):
        there = lax.rem(za + step * pool, na) * nb + xb
        dst = wall.at[core, xb, head, span(p)] if kept else line.at[half, span(p)]
        return remote(
            w_ref.at[span(p)], dst, wz_send.at[step - 1, p], wz_recv.at[step - 1, p], at_chip(there)
        )

    def outward(x, y, p):
        group = lax.rem(head + y, heads_n)
        dst = wall.at[core, xb, head, span(p)]
        src = dst if y == 0 else line.at[group, span(p)]
        return remote(src, dst, wx_send.at[x, y, p], wx_recv.at[x, y, p], at_both(x, y))

    ways = [(x, y) for x in range(nb) for y in range(heads_n) if x or y]

    def over(p):
        part = wall.at[core, :, :, span(p)]
        return remote(part, part, wc_send.at[p], wc_recv.at[p], sibling)

    def stage_one(p):
        for kept in (True, False):

            @pl.when(mine if kept else jnp.logical_not(mine))
            def _(kept=kept):
                for step in range(1, strides):
                    along(step, p, kept).start()

    def stage_two(p):
        for step in range(1, strides):
            along(step, p, True).wait_recv()
        for x, y in ways:
            outward(x, y, p).start()

    def stage_three(p):
        for x, y in ways:
            outward(x, y, p).wait_recv()
        over(p).start()

    stages = (stage_one, stage_two, stage_three)

    end = PIECES + LAG * (len(stages) - 1)
    clock = [0]

    def tick():
        t = clock[0]
        if t >= end:
            return
        clock[0] = t + 1
        for number, stage in enumerate(stages):
            p = t - LAG * number
            if 0 <= p < PIECES:
                stage(p)

    def beat(name, at=0):
        counts = BEATS[name]
        for _ in range(counts[at] if at < len(counts) else 0):
            tick()

    def beats(name, k, first=0, count=na):
        for at in range(first, min(first + count, len(BEATS[name]))):
            if BEATS[name][at]:
                pl.when(k + first == at)(functools.partial(beat, name, at))

    tick()
    beat("start")
    id_copies = [
        remote(ids_ref, ids_all.at[spot, head], id_send.at[d, y], id_recv.at[d, y], at_mate(d, y))
        for d in range(pool)
        for y in range(heads_n)
        if d or y
    ]
    for copy in id_copies:
        copy.start()

    def exchange(phase, g):
        return [
            remote(
                outb.at[phase, g], recvb.at[phase, g],
                ex_send.at[phase, g, 0], ex_recv.at[phase, g, 0], sibling,
            ),
            remote(
                stat.at[phase, 1 - core, g], statr.at[phase, g],
                ex_send.at[phase, g, 1], ex_recv.at[phase, g, 1], sibling,
            ),
        ]

    def side(phase, g, step, number):
        b = lax.rem(xb + step, nb)
        src, dst = ((mb, rxx), (mc, rxxc))[number]
        return remote(
            src.at[phase, g, b], dst.at[phase, g, step],
            sd_send.at[phase, g, step, number], sd_recv.at[phase, g, step, number], at_chip(za * nb + b),
        )

    def deliver(phase, step, number):
        g = lax.rem(za + step, na)
        src, dst = ((mb, rx), (mc, rxc))[number]
        return remote(
            src.at[phase, g, xb], dst.at[phase, step],
            rs_send.at[phase, step, number], rs_recv.at[phase, step, number], at_chip(g * nb + xb),
        )

    def hand_over(phase, g):
        for b in range(nb):
            outb[phase, g, b] = accf[1 - core, g, b].astype(BF16)
        for copy in exchange(phase, g):
            copy.start()

    def send_side(phase, g):
        for step in range(1, nb):
            for number in range(2):
                side(phase, g, step, number).start()

    def wait_side(phase, g):
        for step in range(1, nb):
            for number in range(2):
                side(phase, g, step, number).wait()

    def send_on(phase, g):
        mb[phase, g, xb] = accf[core, g, xb].astype(BF16)
        step = lax.rem(g - za + na, na)

        @pl.when(step != 0)
        def _():
            for number in range(2):
                deliver(phase, step, number).start()

    def places(i):
        for s in range(slices):
            number = i * slices + s
            yield slice(s * rows, (s + 1) * rows), number // CORES, number % CORES

    def tile_of(pieces):
        filled = [None] * STAT
        for at, column in pieces:
            for b in range(blocks):
                filled[at + b] = row_of(column[b * block : (b + 1) * block])
        blank = jnp.zeros((1, LANES), F32)
        return jnp.concatenate([blank if row is None else row for row in filled], axis=0)

    ones = jnp.ones((tokens, LANES), BF16)

    def merge_sums(g):
        for copy in exchange(0, g):
            copy.wait()
        for b in range(nb):
            total = accf[core, g, b] + recvb[0, g, b].astype(F32)
            accf[core, g, b] = total
            mb[0, g, b] = total.astype(BF16)
            mc[0, g, b] = stat[0, core, g, b] + statr[0, g, b]
        send_side(0, g)

    def merge_side_sums(g):
        wait_side(0, g)
        for step in range(1, nb):
            accf[core, g, xb] = accf[core, g, xb] + rxx[0, g, step].astype(F32)
            mc[0, g, xb] = mc[0, g, xb] + rxxc[0, g, step]
        send_on(0, g)

    def sum_group(k, carry):
        g = lax.rem(za + 1 + k, na)
        loads(g, 0).wait()
        for i in range(per):
            member = one_hot(ids_ref[pl.ds(g * per + i, 1), :])
            both = jnp.concatenate([qkv[0, g, :, i * HDIM : (i + 1) * HDIM], ones], axis=1)
            result = jnp.dot(member, both, preferred_element_type=F32)
            for where, b, c in places(i):
                accf[c, g, b] = result[where, :HDIM]
                stat[0, c, g, b] = tile_of([(0, result[where, HDIM:])])
        hand_over(0, g)

        @pl.when(k == 0)
        def _():
            pltpu.make_async_copy(w_ref, line.at[half], own_sem.at[0]).wait()

        beats("sums", k)

        @pl.when(k > 0)
        def _():
            merge_sums(lax.rem(za + k, na))

        @pl.when(k > 1)
        def _():
            merge_side_sums(lax.rem(za + k - 1, na))

        return carry

    lax.fori_loop(0, na, sum_group, 0)
    merge_sums(za)
    merge_side_sums(lax.rem(za + na - 1, na))
    beat("owned")
    merge_side_sums(za)

    for j in range(1, na):
        for number in range(2):
            deliver(0, j, number).wait()
        accf[core, za, xb] = accf[core, za, xb] + rx[0, j].astype(F32)
        mc[0, za, xb] = mc[0, za, xb] + rxc[0, j]
        beat("centre", j - 1)
    for b in range(blocks):
        where = slice(b * block, (b + 1) * block)
        count = columns_of(mc[0, za, xb, b : b + 1, :], block)
        full[chip, core, where, :] = (accf[core, za, xb, where, :] / count).astype(BF16)

    def spread(step):
        part = full.at[chip, core]
        there = lax.rem(za + na - step, na) * nb + xb
        return remote(part, part, ag_send.at[step], ag_recv.at[step], at_chip(there))

    def hop(step, g):
        part = full.at[g * nb + xb, core]
        there = za * nb + lax.rem(xb + step, nb)
        return remote(part, part, hx_send.at[step, g], hx_recv.at[step, g], at_chip(there))

    def share(g):
        part = full.at[pl.ds(g * nb, nb), core]
        return remote(part, part, sib_send.at[g], sib_recv.at[g], sibling)

    def share_group(g):
        for step in range(1, nb):
            hop(step, g).wait_recv()
        share(g).start()

    for step in range(1, nb):
        hop(step, za).start()
    for step in range(1, na):
        spread(step).start()
    beat("spread")
    share_group(za)

    def combine(g, b, left, right, part):
        peak = jnp.maximum(left[:MASS], right[:MASS])
        scale_l = jnp.exp2((left[:MASS] - peak) * SCALE)
        scale_r = jnp.exp2((right[:MASS] - peak) * SCALE)
        mass = left[MASS:] * scale_l + right[MASS:] * scale_r
        mc[1, g, b] = jnp.concatenate([peak, mass], axis=0)
        for x in range(blocks):
            where = slice(x * block, (x + 1) * block)
            total = accf[core, g, b, where, :] * columns_of(scale_l[x : x + 1], block)
            total += part[where].astype(F32) * columns_of(scale_r[x : x + 1], block)
            accf[core, g, b, where, :] = total

    def merge_parts(g):
        for copy in exchange(1, g):
            copy.wait()
        for b in range(nb):
            combine(g, b, stat[1, core, g, b], statr[1, g, b], recvb[1, g, b])
            mb[1, g, b] = accf[core, g, b].astype(BF16)
        send_side(1, g)

    def merge_side_parts(g):
        wait_side(1, g)
        for step in range(1, nb):
            combine(g, xb, mc[1, g, xb], rxxc[1, g, step], rxx[1, g, step])
        send_on(1, g)

    def attend_group(k, carry):
        g = lax.rem(za + k, na)
        following = lax.rem(g + 1, na)

        @pl.when(k + 1 < na)
        def _():
            spread(k + 1).wait_recv()
            for step in range(1, nb):
                hop(step, following).start()

        share(g).wait()
        loads(g, 1).wait()
        loads(g, 2).wait()
        for i in range(per):
            cols = slice(i * HDIM, (i + 1) * HDIM)
            centre = jnp.concatenate([full[g * nb + b, c] for _, b, c in places(i)], axis=0)
            scores = lax.dot_general(
                centre, qkv[1, g, :, cols], (((1,), (1,)), ((), ())), preferred_element_type=F32
            )
            peak = jnp.max(scores, axis=1, keepdims=True)
            weights = jnp.exp2((scores - peak) * SCALE).astype(BF16)
            both = jnp.concatenate([qkv[2, g, :, cols], ones], axis=1)
            result = jnp.dot(weights, both, preferred_element_type=F32)
            peak = jnp.broadcast_to(peak, (CLUSTERS, LANES))
            for where, b, c in places(i):
                accf[c, g, b] = result[where, :HDIM]
                stat[1, c, g, b] = tile_of([(0, peak[where]), (MASS, result[where, HDIM:])])
        hand_over(1, g)
        beats("attend", k)

        @pl.when(k + 1 < na)
        def _():
            share_group(following)

        @pl.when(k > 0)
        def _():
            merge_parts(lax.rem(g - 1 + na, na))

        @pl.when(k > 1)
        def _():
            merge_side_parts(lax.rem(g - 2 + na, na))

        return carry

    lax.fori_loop(0, na, attend_group, 0)
    beat("parts")
    merge_parts(lax.rem(za + na - 1, na))
    if na > 1:
        merge_side_parts(lax.rem(za + na - 2, na))
    merge_side_parts(lax.rem(za + na - 1, na))

    for j in range(1, na):
        deliver(1, j, 1).wait()
    stats = [mc[1, za, xb]] + [rxc[1, j] for j in range(1, na)]
    top = functools.reduce(jnp.maximum, [s[:MASS] for s in stats])
    scales = [jnp.exp2((s[:MASS] - top) * SCALE) for s in stats]
    mass = sum(s[MASS:] * scale for s, scale in zip(stats, scales))
    beat("stats")
    for j in range(na):
        if j > 0:
            deliver(1, j, 0).wait()
        if j > 0:
            beat("merge", j - 1)
        for x in range(blocks):
            where = slice(x * block, (x + 1) * block)
            column = columns_of(scales[j][x : x + 1], block)
            if j == 0:
                accf[core, za, xb, where, :] = accf[core, za, xb, where, :] * column
            else:
                accf[core, za, xb, where, :] += rx[1, j, where, :].astype(F32) * column
    for x in range(blocks):
        where = slice(x * block, (x + 1) * block)
        total = columns_of(mass[x : x + 1], block)
        cev[head, chip, core, where, :] = (accf[core, za, xb, where, :] / total).astype(BF16)

    def spread_out(step):
        part = cev.at[head, chip, core]
        there = lax.rem(za + na - step, na) * nb + xb
        return remote(part, part, a2_send.at[step], a2_recv.at[step], at_chip(there))

    def hop_out(step, g):
        part = cev.at[head, g * nb + xb, core]
        there = za * nb + lax.rem(xb + step, nb)
        return remote(part, part, h2_send.at[step, g], h2_recv.at[step, g], at_chip(there))

    def cross(step, s):
        part = cev.at[head, s, core]
        return remote(part, part, y2_send.at[step - 1, s], y2_recv.at[step - 1, s], at_head(step))

    def share_out(h, s):
        part = cev.at[h, s, core]
        return remote(part, part, s2_send.at[h, s], s2_recv.at[h, s], sibling)

    def pass_on(s):
        for step in range(1, heads_n):
            cross(step, s).start()
        share_out(head, s).start()

    for step in range(1, na):
        spread_out(step).start()
    for step in range(1, nb):
        hop_out(step, za).start()
    pass_on(chip)
    beat("out")
    for k in range(na):
        g = lax.rem(za + k, na)
        if k + 1 < na:
            spread_out(k + 1).wait_recv()
            following = lax.rem(za + k + 1, na)
            for step in range(1, nb):
                hop_out(step, following).start()
            pass_on(following * nb + xb)
        for step in range(1, nb):
            hop_out(step, g).wait_recv()
            pass_on(g * nb + lax.rem(xb - step + nb, nb))
        beat("near", k)

    for copy in id_copies:
        copy.wait()
    own_ids.wait()

    def gather(owner, first, beating, k, carry):
        h, g = lax.rem(head + first + k // na, heads_n), lax.rem(k, na)
        for i in range(per):
            member = one_hot(ids_all[owner, h, pl.ds(g * per + i, 1), :])
            centre = jnp.concatenate([cev[h, g * nb + b, c] for _, b, c in places(i)], axis=0)
            picked = lax.dot_general(member, centre, (((0,), (0,)), ((), ())), preferred_element_type=F32)
            qkv[h, g, :, i * HDIM : (i + 1) * HDIM] = picked.astype(BF16)
        if beating:
            beats("gather", k, first * na, na if first == 0 else (heads_n - 1) * na)
        return carry

    mate = lax.rem(spot + (1 if pool > 1 else 0), pool)

    def held(s, carry):
        share_out(head, s).wait()
        return carry

    lax.fori_loop(0, chips, held, 0)
    lax.fori_loop(0, na, functools.partial(gather, mate, 0, True), 0)
    for j in range(chips):
        s = chip_from(j)
        for step in range(1, heads_n):
            cross(step, s).wait_recv()
            share_out(lax.rem(head - step + heads_n, heads_n), s).start()
        beat("far", j)

    for step in range(1, na):
        spread(step).wait_send()
        spread_out(step).wait_send()
    for g in range(na):
        for step in range(1, nb):
            hop(step, g).wait_send()
            hop_out(step, g).wait_send()

    def settle(s, carry):
        for step in range(1, heads_n):
            share_out(lax.rem(head + step, heads_n), s).wait()
            cross(step, s).wait_send()
        return carry

    lax.fori_loop(0, chips, settle, 0)

    def project(b, c):
        total = None
        for h in range(heads_n):
            term = None
            for g in range(na):
                part = jnp.dot(
                    qkv[h, g], wall[c, b, h, g * width : (g + 1) * width, :],
                    preferred_element_type=F32,
                )
                term = part if term is None else term + part
            term = term.astype(BF16).astype(F32)
            total = term if total is None else total + term
        return total.astype(BF16)

    blocks_n = nb * CORES
    cols = w_ref.shape[1]

    def place_of(k):
        return pl.ds(pl.multiple_of((spot * blocks_n + k) * cols, cols), cols)

    def give(d, k):
        return remote(
            outbox.at[d - 1, k], out_ref.at[:, place_of(k)],
            out_send.at[d - 1, k], out_recv.at[d - 1, k], at_mate(d, 0),
        )

    for d in [*range(1, pool), 0]:
        owner = lax.rem(spot + d, pool)
        leading = d == (1 if pool > 1 else 0)
        first = 1 if leading else 0
        lax.fori_loop(0, (heads_n - first) * na, functools.partial(gather, owner, first, leading), 0)
        if leading:
            while clock[0] < end:
                tick()

            def landed(p, carry):
                over(p).wait_recv()
                return carry

            lax.fori_loop(0, PIECES, landed, 0)

        def column(k, carry, d=d):
            result = project(k // CORES, lax.rem(k, CORES))
            if d == 0:
                out_ref[:, place_of(k)] = result
            else:
                outbox[d - 1, k] = result
                give(d, k).start()
            return carry

        lax.fori_loop(0, blocks_n, column, 0)

    for d in range(1, pool):
        for k in range(blocks_n):
            give(d, k).wait()

    def finish(p, carry):
        for step in range(1, strides):
            along(step, p, True).wait_send()
        for x, y in ways:
            outward(x, y, p).wait_send()
        over(p).wait_send()
        return carry

    lax.fori_loop(0, PIECES, finish, 0)


def local(queries, keys, values, cluster_ids, out_weight):
    n = lax.axis_size("seq")
    heads_n = lax.axis_size("head")
    chips, na, nb = grid_of(n)
    tokens = queries.shape[0]
    heads = queries.shape[1] // HDIM
    rows = heads * CLUSTERS // n
    width = heads // na * HDIM
    depth, cols = out_weight.shape
    pool = na // heads_n
    ids_t = cluster_ids.T

    vmem = pl.BlockSpec(memory_space=pltpu.VMEM)
    anywhere = pl.BlockSpec(memory_space=pl.ANY)
    dma = pltpu.SemaphoreType.DMA

    def pair(*shape):
        shape = tuple(max(size, 1) for size in shape)
        return [dma(shape), dma(shape)]

    blocks_n = CORES * nb
    return pl.pallas_call(
        functools.partial(fused_kernel, n, heads_n),
        out_shape=pltpu.VMEM((tokens, blocks_n * pool * cols), BF16),
        in_specs=[vmem, anywhere, anywhere, anywhere, anywhere],
        out_specs=vmem,
        scratch_shapes=[
            pltpu.VMEM((heads_n, chips, CORES, rows, HDIM), BF16),
            pltpu.VMEM((CORES, nb, heads_n, depth, cols), BF16),
            pltpu.VMEM((pool, heads_n, heads, tokens), jnp.int32),
            pltpu.VMEM((max(pool - 1, 1), blocks_n, tokens, cols), BF16),
            pltpu.VMEM((max(3, heads_n), na, tokens, width), BF16),
            pltpu.VMEM((heads_n, depth, cols), BF16),
            pltpu.VMEM((CORES, na, nb, rows, HDIM), F32),
            pltpu.VMEM((2, CORES, na, nb, STAT, LANES), F32),
            pltpu.VMEM((2, na, nb, rows, HDIM), BF16),
            pltpu.VMEM((2, na, nb, rows, HDIM), BF16),
            pltpu.VMEM((2, na, nb, STAT, LANES), F32),
            pltpu.VMEM((2, na, nb, rows, HDIM), BF16),
            pltpu.VMEM((2, na, nb, STAT, LANES), F32),
            pltpu.VMEM((2, na, nb, rows, HDIM), BF16),
            pltpu.VMEM((2, na, nb, STAT, LANES), F32),
            pltpu.VMEM((2, na, rows, HDIM), BF16),
            pltpu.VMEM((2, na, STAT, LANES), F32),
            pltpu.VMEM((chips, CORES, rows, HDIM), BF16),
            dma((3, na)), dma((2,)),
            *pair(pool, heads_n),
            *pair(2, na, 2), *pair(2, na, nb, 2), *pair(2, na, 2), *pair(chips), *pair(na),
            *pair(chips), *pair(nb, na), *pair(nb, na),
            *pair(heads_n - 1, chips), *pair(heads_n, chips),
            *pair(na // pool - 1, PIECES), *pair(nb, heads_n, PIECES), *pair(PIECES),
            *pair(pool - 1, blocks_n),
        ],
        compiler_params=pltpu.CompilerParams(
            collective_id=0, has_side_effects=True, vmem_limit_bytes=56 << 20
        ),
    )(ids_t, queries, keys, values, out_weight)


def solution(mesh):
    return jax.shard_map(
        local,
        mesh=mesh,
        in_specs=(
            P("seq", "head"),
            P("seq", "head"),
            P("seq", "head"),
            P("seq", "head"),
            P("head", "seq"),
        ),
        out_specs=P("seq", "head"),
        check_vma=False,
    )
```

```python
import functools
import math

import jax
import jax.numpy as jnp
from jax import lax
from jax.experimental import pallas as pl
from jax.experimental.pallas import tpu as pltpu
from jax.sharding import PartitionSpec as P

HDIM = 128
CLUSTERS = 256
LANES = 128
STAT = 8
MASS = 4
CORES = 2
PIECES = 16
LAG = 2
BEATS = {'start': (), 'sums': (0, 1, 0, 1), 'owned': (1,), 'centre': (), 'spread': (2,), 'attend': (1, 1, 1, 1), 'parts': (1,), 'stats': (1,), 'merge': (), 'out': (2,), 'near': (0, 0, 0, 0), 'far': (), 'gather': (1, 1, 1, 1, 1, 1, 1)}
MESH = pl.DeviceIdType.MESH
F32 = jnp.float32
BF16 = jnp.bfloat16
SCALE = math.log2(math.e) / math.sqrt(HDIM)


def grid_of(n):
    chips = n // CORES
    bits = chips.bit_length() - 1
    a = 1 << ((bits + 1) // 2)
    return chips, a, chips // a


def columns_of(row, block):
    return jnp.broadcast_to(row, (LANES, LANES)).T[:block]


def row_of(column):
    block = column.shape[0]
    return jnp.concatenate([column] * (LANES // block), axis=0).T[:1]


def one_hot(ids_row):
    labels = lax.broadcasted_iota(jnp.int32, (CLUSTERS, ids_row.shape[1]), 0).astype(BF16)
    return jnp.where(labels == ids_row.astype(BF16), jnp.ones((), BF16), jnp.zeros((), BF16))


def fused_kernel(
    n, heads_n, ids_ref, q_ref, k_ref, v_ref, w_ref, out_ref,
    cev, wall, ids_all, outbox, qkv, line, accf, stat, outb, recvb, statr, mb, mc, rxx, rxxc, rx, rxc, full,
    load_sem, own_sem, id_send, id_recv, ex_send, ex_recv, sd_send, sd_recv, rs_send, rs_recv, ag_send, ag_recv,
    sib_send, sib_recv, a2_send, a2_recv, hx_send, hx_recv, h2_send, h2_recv, y2_send, y2_recv, s2_send, s2_recv,
    wz_send, wz_recv, wx_send, wx_recv, wc_send, wc_recv, out_send, out_recv,
):
    chips, na, nb = grid_of(n)
    heads, tokens = ids_ref.shape
    per = heads // na
    rows = mb.shape[-2]
    slices = CLUSTERS // rows
    block = min(rows, LANES)
    blocks = rows // block
    width = per * HDIM
    height = w_ref.shape[0] // PIECES
    seq = lax.axis_index("seq")
    head = lax.axis_index("head")
    core = lax.rem(seq, CORES)
    chip = seq // CORES
    za = chip // nb
    xb = lax.rem(chip, nb)
    pool = na // heads_n
    half = za // pool
    spot = lax.rem(za, pool)
    sibling = {"seq": chip * CORES + 1 - core}

    def at_chip(target):
        return {"seq": target * CORES + core}

    def at_head(step):
        return {"head": lax.rem(head + step, heads_n)}

    def at_both(x, y):
        there = za * nb + lax.rem(xb + x, nb)
        return {"seq": there * CORES + core, "head": lax.rem(head + y, heads_n)}

    def at_mate(d, y):
        there = half * pool + lax.rem(spot + d, pool)
        return {"seq": (there * nb + xb) * CORES + core, "head": lax.rem(head + y, heads_n)}

    def remote(src, dst, send, recv, where):
        return pltpu.make_async_remote_copy(
            src_ref=src, dst_ref=dst, send_sem=send, recv_sem=recv, device_id=where, device_id_type=MESH
        )

    def chip_from(j):
        return lax.rem(chip - j + chips, chips)

    def loads(g, number):
        src = (q_ref, k_ref, v_ref)[number]
        return pltpu.make_async_copy(
            src.at[:, pl.ds(pl.multiple_of(g * width, width), width)],
            qkv.at[number, g], load_sem.at[number, g],
        )

    for step in range(1, na + 1):
        loads(lax.rem(za + step, na), 0).start()

    barrier = pltpu.get_barrier_semaphore()
    targets = [sibling]
    targets += [at_chip(lax.rem(za + step, na) * nb + xb) for step in range(1, na)]
    targets += [at_chip(za * nb + lax.rem(xb + step, nb)) for step in range(1, nb)]
    targets += [at_head(step) for step in range(1, heads_n)]
    targets += [at_both(x, y) for x in range(1, nb) for y in range(1, heads_n)]
    targets += [at_mate(d, y) for d in range(1, pool) for y in range(1, heads_n)]
    for target in targets:
        pl.semaphore_signal(barrier, inc=1, device_id=target, device_id_type=MESH)

    own_ids = pltpu.make_async_copy(ids_ref, ids_all.at[spot, head], own_sem.at[1])
    own_ids.start()
    mine = half == head

    @pl.when(mine)
    def _():
        pltpu.make_async_copy(w_ref, wall.at[core, xb, head], own_sem.at[0]).start()

    @pl.when(jnp.logical_not(mine))
    def _():
        pltpu.make_async_copy(w_ref, line.at[half], own_sem.at[0]).start()

    for step in range(na):
        for number in (1, 2):
            loads(lax.rem(za + step, na), number).start()
    pl.semaphore_wait(barrier, len(targets))

    def span(p):
        return pl.ds(p * height, height)

    strides = na // pool

    def along(step, p, kept):
        there = lax.rem(za + step * pool, na) * nb + xb
        dst = wall.at[core, xb, head, span(p)] if kept else line.at[half, span(p)]
        return remote(
            w_ref.at[span(p)], dst, wz_send.at[step - 1, p], wz_recv.at[step - 1, p], at_chip(there)
        )

    def outward(x, y, p):
        group = lax.rem(head + y, heads_n)
        dst = wall.at[core, xb, head, span(p)]
        src = dst if y == 0 else line.at[group, span(p)]
        return remote(src, dst, wx_send.at[x, y, p], wx_recv.at[x, y, p], at_both(x, y))

    ways = [(x, y) for x in range(nb) for y in range(heads_n) if x or y]

    def over(p):
        part = wall.at[core, :, :, span(p)]
        return remote(part, part, wc_send.at[p], wc_recv.at[p], sibling)

    def stage_one(p):
        for kept in (True, False):

            @pl.when(mine if kept else jnp.logical_not(mine))
            def _(kept=kept):
                for step in range(1, strides):
                    along(step, p, kept).start()

    def stage_two(p):
        for step in range(1, strides):
            along(step, p, True).wait_recv()
        for x, y in ways:
            outward(x, y, p).start()

    def stage_three(p):
        for x, y in ways:
            outward(x, y, p).wait_recv()
        over(p).start()

    stages = (stage_one, stage_two, stage_three)

    end = PIECES + LAG * (len(stages) - 1)
    clock = [0]

    def tick():
        t = clock[0]
        if t >= end:
            return
        clock[0] = t + 1
        for number, stage in enumerate(stages):
            p = t - LAG * number
            if 0 <= p < PIECES:
                stage(p)

    def beat(name, at=0):
        counts = BEATS[name]
        for _ in range(counts[at] if at < len(counts) else 0):
            tick()

    def beats(name, k, first=0, count=na):
        for at in range(first, min(first + count, len(BEATS[name]))):
            if BEATS[name][at]:
                pl.when(k + first == at)(functools.partial(beat, name, at))

    tick()
    beat("start")
    id_copies = [
        remote(ids_ref, ids_all.at[spot, head], id_send.at[d, y], id_recv.at[d, y], at_mate(d, y))
        for d in range(pool)
        for y in range(heads_n)
        if d or y
    ]
    for copy in id_copies:
        copy.start()

    def exchange(phase, g):
        return [
            remote(
                outb.at[phase, g], recvb.at[phase, g],
                ex_send.at[phase, g, 0], ex_recv.at[phase, g, 0], sibling,
            ),
            remote(
                stat.at[phase, 1 - core, g], statr.at[phase, g],
                ex_send.at[phase, g, 1], ex_recv.at[phase, g, 1], sibling,
            ),
        ]

    def side(phase, g, step, number):
        b = lax.rem(xb + step, nb)
        src, dst = ((mb, rxx), (mc, rxxc))[number]
        return remote(
            src.at[phase, g, b], dst.at[phase, g, step],
            sd_send.at[phase, g, step, number], sd_recv.at[phase, g, step, number], at_chip(za * nb + b),
        )

    def deliver(phase, step, number):
        g = lax.rem(za + step, na)
        src, dst = ((mb, rx), (mc, rxc))[number]
        return remote(
            src.at[phase, g, xb], dst.at[phase, step],
            rs_send.at[phase, step, number], rs_recv.at[phase, step, number], at_chip(g * nb + xb),
        )

    def hand_over(phase, g):
        for b in range(nb):
            outb[phase, g, b] = accf[1 - core, g, b].astype(BF16)
        for copy in exchange(phase, g):
            copy.start()

    def send_side(phase, g):
        for step in range(1, nb):
            for number in range(2):
                side(phase, g, step, number).start()

    def wait_side(phase, g):
        for step in range(1, nb):
            for number in range(2):
                side(phase, g, step, number).wait()

    def send_on(phase, g):
        mb[phase, g, xb] = accf[core, g, xb].astype(BF16)
        step = lax.rem(g - za + na, na)

        @pl.when(step != 0)
        def _():
            for number in range(2):
                deliver(phase, step, number).start()

    def places(i):
        for s in range(slices):
            number = i * slices + s
            yield slice(s * rows, (s + 1) * rows), number // CORES, number % CORES

    def tile_of(pieces):
        filled = [None] * STAT
        for at, column in pieces:
            for b in range(blocks):
                filled[at + b] = row_of(column[b * block : (b + 1) * block])
        blank = jnp.zeros((1, LANES), F32)
        return jnp.concatenate([blank if row is None else row for row in filled], axis=0)

    ones = jnp.ones((tokens, LANES), BF16)

    def merge_sums(g):
        for copy in exchange(0, g):
            copy.wait()
        for b in range(nb):
            total = accf[core, g, b] + recvb[0, g, b].astype(F32)
            accf[core, g, b] = total
            mb[0, g, b] = total.astype(BF16)
            mc[0, g, b] = stat[0, core, g, b] + statr[0, g, b]
        send_side(0, g)

    def merge_side_sums(g):
        wait_side(0, g)
        for step in range(1, nb):
            accf[core, g, xb] = accf[core, g, xb] + rxx[0, g, step].astype(F32)
            mc[0, g, xb] = mc[0, g, xb] + rxxc[0, g, step]
        send_on(0, g)

    def sum_group(k, carry):
        g = lax.rem(za + 1 + k, na)
        loads(g, 0).wait()
        for i in range(per):
            member = one_hot(ids_ref[pl.ds(g * per + i, 1), :])
            both = jnp.concatenate([qkv[0, g, :, i * HDIM : (i + 1) * HDIM], ones], axis=1)
            result = jnp.dot(member, both, preferred_element_type=F32)
            for where, b, c in places(i):
                accf[c, g, b] = result[where, :HDIM]
                stat[0, c, g, b] = tile_of([(0, result[where, HDIM:])])
        hand_over(0, g)

        @pl.when(k == 0)
        def _():
            pltpu.make_async_copy(w_ref, line.at[half], own_sem.at[0]).wait()

        beats("sums", k)

        @pl.when(k > 0)
        def _():
            merge_sums(lax.rem(za + k, na))

        @pl.when(k > 1)
        def _():
            merge_side_sums(lax.rem(za + k - 1, na))

        return carry

    lax.fori_loop(0, na, sum_group, 0)
    merge_sums(za)
    merge_side_sums(lax.rem(za + na - 1, na))
    beat("owned")
    merge_side_sums(za)

    for j in range(1, na):
        for number in range(2):
            deliver(0, j, number).wait()
        accf[core, za, xb] = accf[core, za, xb] + rx[0, j].astype(F32)
        mc[0, za, xb] = mc[0, za, xb] + rxc[0, j]
        beat("centre", j - 1)
    for b in range(blocks):
        where = slice(b * block, (b + 1) * block)
        count = columns_of(mc[0, za, xb, b : b + 1, :], block)
        full[chip, core, where, :] = (accf[core, za, xb, where, :] / count).astype(BF16)

    def spread(step):
        part = full.at[chip, core]
        there = lax.rem(za + na - step, na) * nb + xb
        return remote(part, part, ag_send.at[step], ag_recv.at[step], at_chip(there))

    def hop(step, g):
        part = full.at[g * nb + xb, core]
        there = za * nb + lax.rem(xb + step, nb)
        return remote(part, part, hx_send.at[step, g], hx_recv.at[step, g], at_chip(there))

    def share(g):
        part = full.at[pl.ds(g * nb, nb), core]
        return remote(part, part, sib_send.at[g], sib_recv.at[g], sibling)

    def share_group(g):
        for step in range(1, nb):
            hop(step, g).wait_recv()
        share(g).start()

    for step in range(1, nb):
        hop(step, za).start()
    for step in range(1, na):
        spread(step).start()
    beat("spread")
    share_group(za)

    def combine(g, b, left, right, part):
        peak = jnp.maximum(left[:MASS], right[:MASS])
        scale_l = jnp.exp2((left[:MASS] - peak) * SCALE)
        scale_r = jnp.exp2((right[:MASS] - peak) * SCALE)
        mass = left[MASS:] * scale_l + right[MASS:] * scale_r
        mc[1, g, b] = jnp.concatenate([peak, mass], axis=0)
        for x in range(blocks):
            where = slice(x * block, (x + 1) * block)
            total = accf[core, g, b, where, :] * columns_of(scale_l[x : x + 1], block)
            total += part[where].astype(F32) * columns_of(scale_r[x : x + 1], block)
            accf[core, g, b, where, :] = total

    def merge_parts(g):
        for copy in exchange(1, g):
            copy.wait()
        for b in range(nb):
            combine(g, b, stat[1, core, g, b], statr[1, g, b], recvb[1, g, b])
            mb[1, g, b] = accf[core, g, b].astype(BF16)
        send_side(1, g)

    def merge_side_parts(g):
        wait_side(1, g)
        for step in range(1, nb):
            combine(g, xb, mc[1, g, xb], rxxc[1, g, step], rxx[1, g, step])
        send_on(1, g)

    def attend_group(k, carry):
        g = lax.rem(za + k, na)
        following = lax.rem(g + 1, na)

        @pl.when(k + 1 < na)
        def _():
            spread(k + 1).wait_recv()
            for step in range(1, nb):
                hop(step, following).start()

        share(g).wait()
        loads(g, 1).wait()
        loads(g, 2).wait()
        for i in range(per):
            cols = slice(i * HDIM, (i + 1) * HDIM)
            centre = jnp.concatenate([full[g * nb + b, c] for _, b, c in places(i)], axis=0)
            scores = lax.dot_general(
                centre, qkv[1, g, :, cols], (((1,), (1,)), ((), ())), preferred_element_type=F32
            )
            peak = jnp.max(scores, axis=1, keepdims=True)
            weights = jnp.exp2((scores - peak) * SCALE).astype(BF16)
            both = jnp.concatenate([qkv[2, g, :, cols], ones], axis=1)
            result = jnp.dot(weights, both, preferred_element_type=F32)
            peak = jnp.broadcast_to(peak, (CLUSTERS, LANES))
            for where, b, c in places(i):
                accf[c, g, b] = result[where, :HDIM]
                stat[1, c, g, b] = tile_of([(0, peak[where]), (MASS, result[where, HDIM:])])
        hand_over(1, g)
        beats("attend", k)

        @pl.when(k + 1 < na)
        def _():
            share_group(following)

        @pl.when(k > 0)
        def _():
            merge_parts(lax.rem(g - 1 + na, na))

        @pl.when(k > 1)
        def _():
            merge_side_parts(lax.rem(g - 2 + na, na))

        return carry

    lax.fori_loop(0, na, attend_group, 0)
    beat("parts")
    merge_parts(lax.rem(za + na - 1, na))
    if na > 1:
        merge_side_parts(lax.rem(za + na - 2, na))
    merge_side_parts(lax.rem(za + na - 1, na))

    for j in range(1, na):
        deliver(1, j, 1).wait()
    stats = [mc[1, za, xb]] + [rxc[1, j] for j in range(1, na)]
    top = functools.reduce(jnp.maximum, [s[:MASS] for s in stats])
    scales = [jnp.exp2((s[:MASS] - top) * SCALE) for s in stats]
    mass = sum(s[MASS:] * scale for s, scale in zip(stats, scales))
    beat("stats")
    for j in range(na):
        if j > 0:
            deliver(1, j, 0).wait()
        if j > 0:
            beat("merge", j - 1)
        for x in range(blocks):
            where = slice(x * block, (x + 1) * block)
            column = columns_of(scales[j][x : x + 1], block)
            if j == 0:
                accf[core, za, xb, where, :] = accf[core, za, xb, where, :] * column
            else:
                accf[core, za, xb, where, :] += rx[1, j, where, :].astype(F32) * column
    for x in range(blocks):
        where = slice(x * block, (x + 1) * block)
        total = columns_of(mass[x : x + 1], block)
        cev[head, chip, core, where, :] = (accf[core, za, xb, where, :] / total).astype(BF16)

    def spread_out(step):
        part = cev.at[head, chip, core]
        there = lax.rem(za + na - step, na) * nb + xb
        return remote(part, part, a2_send.at[step], a2_recv.at[step], at_chip(there))

    def hop_out(step, g):
        part = cev.at[head, g * nb + xb, core]
        there = za * nb + lax.rem(xb + step, nb)
        return remote(part, part, h2_send.at[step, g], h2_recv.at[step, g], at_chip(there))

    def cross(step, s):
        part = cev.at[head, s, core]
        return remote(part, part, y2_send.at[step - 1, s], y2_recv.at[step - 1, s], at_head(step))

    def share_out(h, s):
        part = cev.at[h, s, core]
        return remote(part, part, s2_send.at[h, s], s2_recv.at[h, s], sibling)

    def pass_on(s):
        for step in range(1, heads_n):
            cross(step, s).start()
        share_out(head, s).start()

    for step in range(1, na):
        spread_out(step).start()
    for step in range(1, nb):
        hop_out(step, za).start()
    pass_on(chip)
    beat("out")
    for k in range(na):
        g = lax.rem(za + k, na)
        if k + 1 < na:
            spread_out(k + 1).wait_recv()
            following = lax.rem(za + k + 1, na)
            for step in range(1, nb):
                hop_out(step, following).start()
            pass_on(following * nb + xb)
        for step in range(1, nb):
            hop_out(step, g).wait_recv()
            pass_on(g * nb + lax.rem(xb - step + nb, nb))
        beat("near", k)

    for copy in id_copies:
        copy.wait()
    own_ids.wait()

    def gather(owner, first, beating, k, carry):
        h, g = lax.rem(head + first + k // na, heads_n), lax.rem(k, na)
        for i in range(per):
            member = one_hot(ids_all[owner, h, pl.ds(g * per + i, 1), :])
            centre = jnp.concatenate([cev[h, g * nb + b, c] for _, b, c in places(i)], axis=0)
            picked = lax.dot_general(member, centre, (((0,), (0,)), ((), ())), preferred_element_type=F32)
            qkv[h, g, :, i * HDIM : (i + 1) * HDIM] = picked.astype(BF16)
        if beating:
            beats("gather", k, first * na, na if first == 0 else (heads_n - 1) * na)
        return carry

    mate = lax.rem(spot + (1 if pool > 1 else 0), pool)

    def held(s, carry):
        share_out(head, s).wait()
        return carry

    lax.fori_loop(0, chips, held, 0)
    lax.fori_loop(0, na, functools.partial(gather, mate, 0, True), 0)
    for j in range(chips):
        s = chip_from(j)
        for step in range(1, heads_n):
            cross(step, s).wait_recv()
            share_out(lax.rem(head - step + heads_n, heads_n), s).start()
        beat("far", j)

    for step in range(1, na):
        spread(step).wait_send()
        spread_out(step).wait_send()
    for g in range(na):
        for step in range(1, nb):
            hop(step, g).wait_send()
            hop_out(step, g).wait_send()

    def settle(s, carry):
        for step in range(1, heads_n):
            share_out(lax.rem(head + step, heads_n), s).wait()
            cross(step, s).wait_send()
        return carry

    lax.fori_loop(0, chips, settle, 0)

    def project(b, c, some):
        total = None
        for h in range(heads_n):
            term = None
            for g in range(na):
                part = jnp.dot(
                    qkv[h, g, some], wall[c, b, h, g * width : (g + 1) * width, :],
                    preferred_element_type=F32,
                )
                term = part if term is None else term + part
            term = term.astype(BF16).astype(F32)
            total = term if total is None else total + term
        return total.astype(BF16)

    blocks_n = nb * CORES
    cols = w_ref.shape[1]

    halves = (pl.ds(0, tokens // 2), pl.ds(tokens // 2, tokens // 2))

    def place_of(k):
        return pl.ds(pl.multiple_of((spot * blocks_n + k) * cols, cols), cols)

    def give(d, k, piece):
        return remote(
            outbox.at[d - 1, k, halves[piece]], out_ref.at[halves[piece], place_of(k)],
            out_send.at[d - 1, k, piece], out_recv.at[d - 1, k, piece], at_mate(d, 0),
        )

    for d in [*range(1, pool), 0]:
        owner = lax.rem(spot + d, pool)
        leading = d == (1 if pool > 1 else 0)
        first = 1 if leading else 0
        lax.fori_loop(0, (heads_n - first) * na, functools.partial(gather, owner, first, leading), 0)
        if leading:
            while clock[0] < end:
                tick()

            def landed(p, carry):
                over(p).wait_recv()
                return carry

            lax.fori_loop(0, PIECES, landed, 0)

        def column(k, carry, d=d):
            for piece in range(2):
                result = project(k // CORES, lax.rem(k, CORES), halves[piece])
                if d == 0:
                    out_ref[halves[piece], place_of(k)] = result
                else:
                    outbox[d - 1, k, halves[piece]] = result
                    give(d, k, piece).start()
            return carry

        lax.fori_loop(0, blocks_n, column, 0)

    for d in range(1, pool):
        for k in range(blocks_n):
            for piece in range(2):
                give(d, k, piece).wait()

    def finish(p, carry):
        for step in range(1, strides):
            along(step, p, True).wait_send()
        for x, y in ways:
            outward(x, y, p).wait_send()
        over(p).wait_send()
        return carry

    lax.fori_loop(0, PIECES, finish, 0)


def local(queries, keys, values, cluster_ids, out_weight):
    n = lax.axis_size("seq")
    heads_n = lax.axis_size("head")
    chips, na, nb = grid_of(n)
    tokens = queries.shape[0]
    heads = queries.shape[1] // HDIM
    rows = heads * CLUSTERS // n
    width = heads // na * HDIM
    depth, cols = out_weight.shape
    pool = na // heads_n
    ids_t = cluster_ids.T

    vmem = pl.BlockSpec(memory_space=pltpu.VMEM)
    anywhere = pl.BlockSpec(memory_space=pl.ANY)
    dma = pltpu.SemaphoreType.DMA

    def pair(*shape):
        shape = tuple(max(size, 1) for size in shape)
        return [dma(shape), dma(shape)]

    blocks_n = CORES * nb
    return pl.pallas_call(
        functools.partial(fused_kernel, n, heads_n),
        out_shape=pltpu.VMEM((tokens, blocks_n * pool * cols), BF16),
        in_specs=[vmem, anywhere, anywhere, anywhere, anywhere],
        out_specs=vmem,
        scratch_shapes=[
            pltpu.VMEM((heads_n, chips, CORES, rows, HDIM), BF16),
            pltpu.VMEM((CORES, nb, heads_n, depth, cols), BF16),
            pltpu.VMEM((pool, heads_n, heads, tokens), jnp.int32),
            pltpu.VMEM((max(pool - 1, 1), blocks_n, tokens, cols), BF16),
            pltpu.VMEM((max(3, heads_n), na, tokens, width), BF16),
            pltpu.VMEM((heads_n, depth, cols), BF16),
            pltpu.VMEM((CORES, na, nb, rows, HDIM), F32),
            pltpu.VMEM((2, CORES, na, nb, STAT, LANES), F32),
            pltpu.VMEM((2, na, nb, rows, HDIM), BF16),
            pltpu.VMEM((2, na, nb, rows, HDIM), BF16),
            pltpu.VMEM((2, na, nb, STAT, LANES), F32),
            pltpu.VMEM((2, na, nb, rows, HDIM), BF16),
            pltpu.VMEM((2, na, nb, STAT, LANES), F32),
            pltpu.VMEM((2, na, nb, rows, HDIM), BF16),
            pltpu.VMEM((2, na, nb, STAT, LANES), F32),
            pltpu.VMEM((2, na, rows, HDIM), BF16),
            pltpu.VMEM((2, na, STAT, LANES), F32),
            pltpu.VMEM((chips, CORES, rows, HDIM), BF16),
            dma((3, na)), dma((2,)),
            *pair(pool, heads_n),
            *pair(2, na, 2), *pair(2, na, nb, 2), *pair(2, na, 2), *pair(chips), *pair(na),
            *pair(chips), *pair(nb, na), *pair(nb, na),
            *pair(heads_n - 1, chips), *pair(heads_n, chips),
            *pair(na // pool - 1, PIECES), *pair(nb, heads_n, PIECES), *pair(PIECES),
            *pair(pool - 1, blocks_n, 2),
        ],
        compiler_params=pltpu.CompilerParams(
            collective_id=0, has_side_effects=True, vmem_limit_bytes=56 << 20
        ),
    )(ids_t, queries, keys, values, out_weight)


def solution(mesh):
    return jax.shard_map(
        local,
        mesh=mesh,
        in_specs=(
            P("seq", "head"),
            P("seq", "head"),
            P("seq", "head"),
            P("seq", "head"),
            P("head", "seq"),
        ),
        out_specs=P("seq", "head"),
        check_vma=False,
    )
```
